256 devices in a mesh: rows: 4 (over y), cand: 64 (over x, z, core).
Axes of the slice: x: 4, y: 4, z: 8, core: 2. Of those that a mesh axis runs over, the one named last changes fastest.
Arguments:
- whitened: float32 [256, 2048], P('cand', 'rows'), may hold values from -6 to 6
- factor_rows: float32 [2048, 2048], P('rows'), as said below
- diag_inv: float32 [2048, 512], P('rows'), as said below
- observed: float32 [22, 2048], P(None, 'rows'), may hold values from 0 to 1
- inv_length: float32 [22], replicated, may hold values from 0.4 to 2
- grid_coords: int32 [22, 262144], P(None, 'cand'), may hold values from 0 to 20
- frequencies: float32 [22, 8192], P(None, 'rows'), may hold values from -8 to 8
- phases: float32 [8192], P('rows'), may hold values from -3.140625 to 3.140625
- prior_coef: bfloat16 [256, 8192], P('cand', 'rows'), may hold values from -6 to 6
Outputs:
- samples_at: float32 [262144, 256], P('cand', 'rows')
The draws below stay inside these ranges and needn't reach their ends.
Inputs may be any that keep to these rules, and one draw needn't show every extreme that they name: `factor_rows`: entries in and above the diagonal blocks of 512 x 512 are zero. `diag_inv`: each block of 512 rows is lower triangular with a positive diagonal.
All inputs are finite; a program needn't handle non-finite values.
Results may differ from the reference program's by a relative error of at most 0.004.
Values may be sent and summed in bfloat16 or wider, within the bound.
No kernel may reach another device: no remote copies, remote signals or barrier semaphores. Data moves between devices by JAX's collectives and lax.ppermute only.
A program may use at most 320 MiB of HBM per device.

```python
import math
import jax
import jax.numpy as jnp
from jax import lax

DIM = 22
FEAT = 8192
SAMPLES = 256
BLOCK = 512
GRID = 21
CAND_DEV = 4096
OBS = 2048
CANDS = 262144


def draw_factor_rows(key, part):
    row_block = jnp.arange(OBS)[:, None] // BLOCK
    col_block = jnp.arange(OBS)[None, :] // BLOCK
    below = (row_block > col_block).astype(jnp.float32)
    values = jax.random.uniform(key, (OBS, OBS), jnp.float32, -0.8, 0.8)
    return values * below / jnp.sqrt(jnp.float32(OBS))


def draw_diag_inv(key, part):
    first_key, second_key = jax.random.split(key)
    row_local = jnp.arange(OBS)[:, None] % BLOCK
    column = jnp.arange(BLOCK)[None, :]
    lower = (column < row_local).astype(jnp.float32)
    on_diagonal = column == row_local
    spread = jax.random.uniform(first_key, (OBS, BLOCK), jnp.float32, -0.8, 0.8) / jnp.sqrt(jnp.float32(BLOCK))
    leading = jax.random.uniform(second_key, (OBS, BLOCK), jnp.float32, 0.6, 1.2)
    return spread * lower + jnp.where(on_diagonal, leading, 0.0)


def set_ends(values, rng, smallest, high):
    spot = [jax.random.randint(jax.random.fold_in(rng, axis), (), 0, length) for axis, length in enumerate(values.shape)]
    longest = values.shape.index(max(values.shape))
    neighbour = spot[:longest] + [(spot[longest] + 1) % values.shape[longest]] + spot[longest + 1:]
    return values.at[tuple(spot)].set(smallest).at[tuple(neighbour)].set(high)


def shard_levels(stream_key, extent, cuts, low, high):
    factor_of = 1.0
    for position, blocks in cuts:
        heights = jax.random.uniform(jax.random.fold_in(jax.random.fold_in(stream_key, 6), position), (blocks,), jnp.float32, low / len(cuts), high / len(cuts))
        factor_of = factor_of * jnp.repeat(jnp.exp(heights), extent[position] // blocks).reshape((-1,) + (1,) * (len(extent) - 1 - position))
    return factor_of


def centred(own_key, shape, deviation, bound, cuts=(), held_as=jnp.bfloat16):
    array = jax.random.normal(own_key, shape, jnp.float32) * deviation
    if len(cuts) > 0:
        array = shard_levels(own_key, shape, cuts, -0.22, 0.18) * array
    return jnp.clip(array, min=-bound, max=bound).astype(held_as)


def setup_inputs(seed: int = 0) -> dict:
    key_of = jax.random.split(jax.random.key(seed), 10)
    return {
        "whitened": centred(key_of[0], (SAMPLES, OBS), 1.0, 6.0, ((0, 64), (1, 4)), jnp.float32),
        "factor_rows": draw_factor_rows(jax.random.fold_in(key_of[9], 71), 0),
        "diag_inv": draw_diag_inv(jax.random.fold_in(key_of[9], 71), 0),
        "observed": jnp.clip(1.0 * jax.random.uniform(key_of[3], (DIM, OBS), jnp.float32) ** shard_levels(key_of[3], (DIM, OBS), ((1, 4),), -0.2, 0.2), 0.0, 1.0),
        "inv_length": jnp.clip(jnp.exp(jax.random.uniform(key_of[4], (DIM,), jnp.float32, math.log(0.4), math.log(2.0))), 0.4, 2.0),
        "grid_coords": set_ends(jax.random.randint(key_of[5], (DIM, CANDS), 0, GRID), jax.random.fold_in(key_of[5], 1), 0, GRID - 1).astype(jnp.int32),
        "frequencies": centred(key_of[6], (DIM, FEAT), 2.0, 8.0, ((1, 4),), jnp.float32),
        "phases": jnp.clip(jax.random.uniform(key_of[7], (FEAT,), jnp.float32, -3.140625, 3.140625), -3.140625, 3.140625),
        "prior_coef": centred(key_of[8], (SAMPLES, FEAT), 1.0, 6.0, ((0, 64), (1, 4))),
    }


def back_solve(whitened, factor_rows, diag_inv):
    carried = jnp.zeros_like(whitened)
    pieces = []
    for block_id in reversed(range(OBS // BLOCK)):
        offset = block_id * BLOCK
        remaining = whitened[:, offset:offset + BLOCK] - carried[:, offset:offset + BLOCK]
        solved = jnp.dot(remaining, diag_inv[offset:offset + BLOCK], precision=lax.Precision.HIGHEST, preferred_element_type=jnp.float32)
        carried = carried + jnp.dot(solved, factor_rows[offset:offset + BLOCK], precision=lax.Precision.HIGHEST, preferred_element_type=jnp.float32)
        pieces.append(solved)
    return jnp.concatenate(pieces[::-1], axis=1)

def evaluate_block(coords_block, weights_wire, observed, inv_length, frequencies, phases, prior_coef):
    mixture = coords_block.astype(jnp.float32) / (GRID - 1)
    angles = jnp.dot(mixture.T, frequencies, precision=lax.Precision.HIGHEST, preferred_element_type=jnp.float32) + phases[None, :]
    features_map = (jnp.sqrt(2.0 / FEAT) * jnp.cos(angles)).astype(jnp.bfloat16)
    prior_part = jnp.dot(features_map, prior_coef.T, preferred_element_type=jnp.float32)
    squared = jnp.zeros((mixture.shape[1], observed.shape[1]), jnp.float32)
    for column in range(DIM):
        gap = (mixture[column][:, None] - observed[column][None, :]) * inv_length[column]
        squared = squared + gap * gap
    kernel_tile = jnp.exp(-0.5 * squared).astype(jnp.bfloat16)
    return prior_part + jnp.dot(kernel_tile, weights_wire.T, preferred_element_type=jnp.float32)

def reference(whitened, factor_rows, diag_inv, observed, inv_length, grid_coords, frequencies, phases, prior_coef):
    weights = back_solve(whitened, factor_rows, diag_inv)
    weights_wire = weights.astype(jnp.bfloat16)
    blocked = jnp.transpose(grid_coords.reshape(DIM, CANDS // CAND_DEV, CAND_DEV), (1, 0, 2))

    def one_block(coords_block):
        return evaluate_block(coords_block, weights_wire, observed, inv_length, frequencies, phases, prior_coef)
    values = lax.map(one_block, blocked)
    return values.reshape(CANDS, SAMPLES)
```

```python
import jax
import jax.numpy as jnp
from jax import lax
from jax.experimental import pallas as pl
from jax.experimental.pallas import tpu as pltpu
from jax.sharding import PartitionSpec as P

F32 = jnp.float32
BF16 = jnp.bfloat16
GRID = 21
DIM = 22
CORES = 2
DEPTHS = 8
WIDTHS = 4
LANES = 128
STRIPE = 24
ROW_CHUNK = 256
CAND_TILE = 256
CHUNKS = 8
PARTS = 2
VMEM_BYTES = 16 * 2**20
LOG2E = 1.4426950408889634
INV_TURN = 0.15915494309189535
SINE = (0.55535848, -0.91343016, 0.4493464, -0.09804192)


def params(limit=VMEM_BYTES):
    return pltpu.CompilerParams(vmem_limit_bytes=limit)


def whole():
    return pl.BlockSpec(memory_space=pltpu.VMEM)


def three_pieces(values):
    high = values.astype(BF16).astype(F32)
    rest = values - high
    middle = rest.astype(BF16).astype(F32)
    return high, middle, (rest - middle).astype(BF16).astype(F32)


def stack_pieces(scratch, values, tail):
    scratch[...] = jnp.zeros_like(scratch)
    for piece, part in enumerate(values):
        scratch[piece * STRIPE : piece * STRIPE + DIM, :] = part
    row = lax.broadcasted_iota(jnp.int32, (8, scratch.shape[1]), 0)
    block = jnp.zeros((8, scratch.shape[1]), F32)
    for index, line in enumerate(tail):
        block = jnp.where(row == index, line, block)
    scratch[3 * STRIPE : 3 * STRIPE + 8, :] = block


def prepare_kernel(
    freq_ref, phase_ref, observed_ref, scale_ref, grid_ref,
    turns_ref, exponent_ref, levels_ref, wide, narrow, tall,
):
    stack_pieces(
        wide,
        three_pieces(freq_ref[...] * (INV_TURN / (GRID - 1))),
        three_pieces(phase_ref[...] * INV_TURN),
    )
    for start in range(0, wide.shape[1], 512):
        turns_ref[start : start + 512, :] = wide[:, start : start + 512].T.astype(BF16)
    squares = scale_ref[...] * scale_ref[...]
    observed = observed_ref[...]
    ones = jnp.ones((1, narrow.shape[1]), F32)
    norm = jnp.sum(observed * observed * squares, axis=0, keepdims=True) * (-0.5 * LOG2E)
    stack_pieces(
        narrow,
        three_pieces(observed * squares * (LOG2E / (GRID - 1))),
        three_pieces(norm) + (ones, ones, ones),
    )
    exponent_ref[...] = narrow[...].T.astype(BF16)
    levels = grid_ref[...].astype(F32)
    ones = jnp.ones((1, tall.shape[1]), F32)
    norm = jnp.sum(levels * levels * squares, axis=0, keepdims=True) * (
        -0.5 * LOG2E / (GRID - 1) ** 2
    )
    stack_pieces(tall, (levels, levels, levels), (ones, ones, ones) + three_pieces(norm))
    levels_ref[...] = tall[...].astype(BF16)


def prepare(frequencies, phases, observed, inv_length, grid_coords):
    feats, obs, cands = frequencies.shape[1], observed.shape[1], grid_coords.shape[1]
    return pl.pallas_call(
        prepare_kernel,
        out_shape=(
            jax.ShapeDtypeStruct((feats, LANES), BF16),
            jax.ShapeDtypeStruct((obs, LANES), BF16),
            jax.ShapeDtypeStruct((LANES, cands), BF16),
        ),
        in_specs=[whole()] * 5,
        out_specs=(whole(),) * 3,
        scratch_shapes=[
            pltpu.VMEM((LANES, feats), F32),
            pltpu.VMEM((LANES, obs), F32),
            pltpu.VMEM((LANES, cands), F32),
        ],
        compiler_params=params(),
        cost_estimate=pl.CostEstimate(flops=10**7, transcendentals=0, bytes_accessed=4 * 2**20),
        name="prepare",
    )(frequencies, phases[None, :], observed, inv_length[:, None], grid_coords)


def cosine(turns):
    near = turns - jnp.round(turns)
    square = near * near
    poly = ((SINE[3] * square + SINE[2]) * square + SINE[1]) * square + SINE[0]
    sine = near * poly
    return (0.015625 - sine * sine).astype(BF16)


def tile_kernel(turns_ref, exponent_ref, levels_ref, features_ref, kernel_ref):
    levels = levels_ref[...]
    for start in range(0, turns_ref.shape[0], ROW_CHUNK):
        rows = slice(start, start + ROW_CHUNK)
        turns = jnp.dot(turns_ref[rows, :], levels, preferred_element_type=F32)
        features_ref[rows, :] = cosine(turns)
    for start in range(0, exponent_ref.shape[0], ROW_CHUNK):
        rows = slice(start, start + ROW_CHUNK)
        exponent = jnp.dot(exponent_ref[rows, :], levels, preferred_element_type=F32)
        kernel_ref[rows, :] = jnp.exp2(exponent).astype(BF16)


def tiles(turns, exponent, levels, chunk):
    feats, obs = turns.shape[0], exponent.shape[0]
    cands = levels.shape[1] // CHUNKS
    steps = cands // CAND_TILE
    return pl.pallas_call(
        tile_kernel,
        out_shape=(
            jax.ShapeDtypeStruct((feats, cands), BF16),
            jax.ShapeDtypeStruct((obs, cands), BF16),
        ),
        grid=(steps,),
        in_specs=[
            whole(),
            whole(),
            pl.BlockSpec((LANES, CAND_TILE), lambda i: (0, i + chunk * steps)),
        ],
        out_specs=(
            pl.BlockSpec((feats, CAND_TILE), lambda i: (0, i)),
            pl.BlockSpec((obs, CAND_TILE), lambda i: (0, i)),
        ),
        compiler_params=params(),
        cost_estimate=pl.CostEstimate(
            flops=24 * (feats + obs) * cands,
            transcendentals=obs * cands,
            bytes_accessed=2 * (feats + obs) * cands,
        ),
    )(turns, exponent, levels)


def order_kernel(place_ref, near_ref, far_ref, out_ref):
    rows, half = out_ref.shape[0], near_ref.shape[0]
    block = rows // WIDTHS
    row = lax.broadcasted_iota(jnp.int32, (rows, half), 0)
    column = lax.broadcasted_iota(jnp.int32, (rows, half), 1)
    sample = (row + place_ref[0] * block) & (rows - 1)
    shard = rows // (WIDTHS * DEPTHS * CORES)
    offset = (sample // shard) ^ place_ref[1]
    pieces = WIDTHS * DEPTHS
    source = (offset // CORES + (offset & (CORES - 1)) * pieces) * shard + (sample & (shard - 1))
    near = (source == column).astype(F32).astype(BF16)
    far = (source == column + half).astype(F32).astype(BF16)
    step = 512
    for start in range(0, out_ref.shape[1], step):
        cols = slice(start, start + step)
        out_ref[:, cols] = (
            jnp.dot(near, near_ref[:, cols], preferred_element_type=F32)
            + jnp.dot(far, far_ref[:, cols], preferred_element_type=F32)
        ).astype(BF16)


def in_order(place, near, far):
    return pl.pallas_call(
        order_kernel,
        out_shape=jax.ShapeDtypeStruct((2 * near.shape[0], near.shape[1]), BF16),
        in_specs=[pl.BlockSpec(memory_space=pltpu.SMEM), whole(), whole()],
        out_specs=whole(),
        compiler_params=params(),
        cost_estimate=pl.CostEstimate(
            flops=4 * near.shape[0] ** 2 * near.shape[1] * 2,
            transcendentals=0,
            bytes_accessed=8 * near.size,
        ),
    )(place, near, far)


def product_kernel(coef_ref, weight_ref, *refs):
    count = (len(refs) - WIDTHS) // 2
    features, kernels, outs = refs[:count], refs[count : 2 * count], refs[2 * count :]
    block = coef_ref.shape[0] // WIDTHS
    for chunk in range(count):
        @pl.when(pl.program_id(0) == chunk)
        def _(chunk=chunk):
            total = jnp.dot(coef_ref[...], features[chunk][...], preferred_element_type=F32)
            total = total + jnp.dot(
                weight_ref[...], kernels[chunk][...], preferred_element_type=F32
            )
            for target, out in enumerate(outs):
                out[...] = total[target * block : (target + 1) * block].astype(out.dtype)


def products(coefs, weights, features, kernels):
    count, cands = len(features), features[0].shape[1]
    block = coefs.shape[0] // WIDTHS
    feats, obs = features[0].shape[0], kernels[0].shape[0]
    shape = (block, count * cands)
    out_shapes = (jax.ShapeDtypeStruct(shape, F32),) + (jax.ShapeDtypeStruct(shape, BF16),) * (
        WIDTHS - 1
    )
    return pl.pallas_call(
        product_kernel,
        out_shape=out_shapes,
        grid=(count,),
        in_specs=[whole(), whole()]
        + [pl.BlockSpec((feats, cands), lambda i: (0, 0))] * count
        + [pl.BlockSpec((obs, cands), lambda i: (0, 0))] * count,
        out_specs=tuple(pl.BlockSpec((block, cands), lambda i: (0, i)) for _ in out_shapes),
        compiler_params=params(40 * 2**20),
        cost_estimate=pl.CostEstimate(
            flops=2 * coefs.shape[0] * (feats + obs) * count * cands,
            transcendentals=0,
            bytes_accessed=2 * (feats + obs) * count * cands,
        ),
    )(coefs, weights, *features, *kernels)


def exchange_pairs(mask):
    devices = WIDTHS * DEPTHS * CORES
    return [(i, i ^ mask) for i in range(devices)]


def spread(piece):
    def swap(held, mask):
        return lax.ppermute(held, "cand", exchange_pairs(mask))

    held = piece
    for hop in (1, 2, 4):
        other = swap(held, hop * CORES)
        held = lax.optimization_barrier(jnp.concatenate([held, other], axis=0))
    others = [swap(held, hop * DEPTHS * CORES) for hop in range(1, WIDTHS)]
    held = lax.optimization_barrier(jnp.concatenate([held] + others, axis=0))
    return held, swap(held, 1)


def exact_dot(left, right):
    return jnp.dot(
        left, right, precision=lax.Precision.HIGHEST, preferred_element_type=jnp.float32
    )


def solve_chain(whitened, factor_rows, diag_inv):
    sections = lax.axis_size("rows")
    position = lax.axis_index("rows")
    width = diag_inv.shape[1]
    weights = jnp.zeros_like(whitened)
    carried = None
    for section in reversed(range(sections)):
        earlier = section * width

        def solve_own(carried, weights):
            remaining = whitened if carried is None else whitened - carried[:, earlier:]
            solved = exact_dot(remaining, diag_inv)
            if section == 0:
                return None, solved
            update = exact_dot(solved, factor_rows[:, :earlier])
            if carried is not None:
                update = carried[:, :earlier] + update
            return update, solved

        def pass_on(carried, weights):
            if section == 0:
                return None, weights
            shape = (whitened.shape[0], earlier)
            return (jnp.zeros(shape, jnp.float32) if carried is None else carried[:, :earlier]), weights

        carried, weights = lax.cond(position == section, solve_own, pass_on, carried, weights)
        if section > 0:
            pairs = [(section, section - 1)]
            carried = lax.ppermute(carried, "rows", pairs)
    return weights


def body(
    whitened,
    factor_rows,
    diag_inv,
    observed,
    inv_length,
    grid_coords,
    frequencies,
    phases,
    prior_coef,
):
    place = jnp.stack([lax.axis_index("rows"), lax.axis_index("cand")]).astype(jnp.int32)
    coef_near, coef_far = spread(prior_coef)
    weights = solve_chain(whitened, factor_rows, diag_inv).astype(BF16)
    weight_near, weight_far = spread(weights)
    turns, exponent, levels = prepare(frequencies, phases, observed, inv_length, grid_coords)
    made = [tiles(turns, exponent, levels, chunk) for chunk in range(CHUNKS)]
    coefs = in_order(place, coef_near, coef_far)
    solved = in_order(place, weight_near, weight_far)
    rows = lax.axis_size("rows")
    each = CHUNKS // PARTS
    sums = []
    for part in range(PARTS):
        mine = made[part * each : (part + 1) * each]
        own, *away = products(coefs, solved, [m[0] for m in mine], [m[1] for m in mine])
        total = own
        for shift, block in enumerate(away, 1):
            pairs = [(i, (i + shift) % rows) for i in range(rows)]
            total = total + lax.ppermute(block, "rows", pairs).astype(F32)
        sums.append(total)
    return jnp.concatenate(sums, axis=1).T


def solution(mesh):
    in_specs = (
        P("cand", "rows"),
        P("rows", None),
        P("rows", None),
        P(None, "rows"),
        P(),
        P(None, "cand"),
        P(None, "rows"),
        P("rows"),
        P("cand", "rows"),
    )
    out_specs = P("cand", "rows")

    return jax.shard_map(body, mesh=mesh, in_specs=in_specs, out_specs=out_specs, check_vma=False)
```

```python
import jax
import jax.numpy as jnp
from jax import lax
from jax.experimental import pallas as pl
from jax.experimental.pallas import tpu as pltpu
from jax.sharding import PartitionSpec as P

F32 = jnp.float32
BF16 = jnp.bfloat16
GRID = 21
DIM = 22
CORES = 2
DEPTHS = 8
WIDTHS = 4
LANES = 128
STRIPE = 24
ROW_CHUNK = 256
CAND_TILE = 256
CHUNKS = 8
PARTS = 2
VMEM_BYTES = 16 * 2**20
LOG2E = 1.4426950408889634
INV_TURN = 0.15915494309189535
SINE = (0.55535848, -0.91343016, 0.4493464, -0.09804192)


def params(limit=VMEM_BYTES):
    return pltpu.CompilerParams(vmem_limit_bytes=limit)


def whole():
    return pl.BlockSpec(memory_space=pltpu.VMEM)


def three_pieces(values):
    high = values.astype(BF16).astype(F32)
    rest = values - high
    middle = rest.astype(BF16).astype(F32)
    return high, middle, (rest - middle).astype(BF16).astype(F32)


def stack_pieces(scratch, values, tail):
    scratch[...] = jnp.zeros_like(scratch)
    for piece, part in enumerate(values):
        scratch[piece * STRIPE : piece * STRIPE + DIM, :] = part
    row = lax.broadcasted_iota(jnp.int32, (8, scratch.shape[1]), 0)
    block = jnp.zeros((8, scratch.shape[1]), F32)
    for index, line in enumerate(tail):
        block = jnp.where(row == index, line, block)
    scratch[3 * STRIPE : 3 * STRIPE + 8, :] = block


def prepare_kernel(
    freq_ref, phase_ref, observed_ref, scale_ref, grid_ref,
    turns_ref, exponent_ref, levels_ref, wide, narrow, tall,
):
    stack_pieces(
        wide,
        three_pieces(freq_ref[...] * (INV_TURN / (GRID - 1))),
        three_pieces(phase_ref[...] * INV_TURN),
    )
    for start in range(0, wide.shape[1], 512):
        turns_ref[start : start + 512, :] = wide[:, start : start + 512].T.astype(BF16)
    scale = jnp.broadcast_to(scale_ref[...], (DIM, DIM))
    line = lax.broadcasted_iota(jnp.int32, (DIM, DIM), 0)
    lane = lax.broadcasted_iota(jnp.int32, (DIM, DIM), 1)
    scale = jnp.sum(jnp.where(line == lane, scale, 0.0), axis=1, keepdims=True)
    squares = scale * scale
    observed = observed_ref[...]
    ones = jnp.ones((1, narrow.shape[1]), F32)
    norm = jnp.sum(observed * observed * squares, axis=0, keepdims=True) * (-0.5 * LOG2E)
    stack_pieces(
        narrow,
        three_pieces(observed * squares * (LOG2E / (GRID - 1))),
        three_pieces(norm) + (ones, ones, ones),
    )
    exponent_ref[...] = narrow[...].T.astype(BF16)
    levels = grid_ref[...].astype(F32)
    ones = jnp.ones((1, tall.shape[1]), F32)
    norm = jnp.sum(levels * levels * squares, axis=0, keepdims=True) * (
        -0.5 * LOG2E / (GRID - 1) ** 2
    )
    stack_pieces(tall, (levels, levels, levels), (ones, ones, ones) + three_pieces(norm))
    levels_ref[...] = tall[...].astype(BF16)


def prepare(frequencies, phases, observed, inv_length, grid_coords):
    feats, obs, cands = frequencies.shape[1], observed.shape[1], grid_coords.shape[1]
    return pl.pallas_call(
        prepare_kernel,
        out_shape=(
            jax.ShapeDtypeStruct((feats, LANES), BF16),
            jax.ShapeDtypeStruct((obs, LANES), BF16),
            jax.ShapeDtypeStruct((LANES, cands), BF16),
        ),
        in_specs=[whole()] * 5,
        out_specs=(whole(),) * 3,
        scratch_shapes=[
            pltpu.VMEM((LANES, feats), F32),
            pltpu.VMEM((LANES, obs), F32),
            pltpu.VMEM((LANES, cands), F32),
        ],
        compiler_params=params(),
        cost_estimate=pl.CostEstimate(flops=10**7, transcendentals=0, bytes_accessed=4 * 2**20),
        name="prepare",
    )(frequencies, phases[None, :], observed, inv_length[None, :], grid_coords)


def cosine(turns):
    near = turns - jnp.round(turns)
    square = near * near
    poly = ((SINE[3] * square + SINE[2]) * square + SINE[1]) * square + SINE[0]
    sine = near * poly
    return (0.015625 - sine * sine).astype(BF16)


def tile_kernel(turns_ref, exponent_ref, levels_ref, features_ref, kernel_ref):
    levels = levels_ref[...]
    for start in range(0, turns_ref.shape[0], ROW_CHUNK):
        rows = slice(start, start + ROW_CHUNK)
        turns = jnp.dot(turns_ref[rows, :], levels, preferred_element_type=F32)
        features_ref[rows, :] = cosine(turns)
    for start in range(0, exponent_ref.shape[0], ROW_CHUNK):
        rows = slice(start, start + ROW_CHUNK)
        exponent = jnp.dot(exponent_ref[rows, :], levels, preferred_element_type=F32)
        kernel_ref[rows, :] = jnp.exp2(exponent).astype(BF16)


def tiles(turns, exponent, levels, chunk):
    feats, obs = turns.shape[0], exponent.shape[0]
    cands = levels.shape[1] // CHUNKS
    steps = cands // CAND_TILE
    return pl.pallas_call(
        tile_kernel,
        out_shape=(
            jax.ShapeDtypeStruct((feats, cands), BF16),
            jax.ShapeDtypeStruct((obs, cands), BF16),
        ),
        grid=(steps,),
        in_specs=[
            whole(),
            whole(),
            pl.BlockSpec((LANES, CAND_TILE), lambda i: (0, i + chunk * steps)),
        ],
        out_specs=(
            pl.BlockSpec((feats, CAND_TILE), lambda i: (0, i)),
            pl.BlockSpec((obs, CAND_TILE), lambda i: (0, i)),
        ),
        compiler_params=params(),
        cost_estimate=pl.CostEstimate(
            flops=24 * (feats + obs) * cands,
            transcendentals=obs * cands,
            bytes_accessed=2 * (feats + obs) * cands,
        ),
    )(turns, exponent, levels)


def choice_kernel(place_ref, out_ref):
    rows = out_ref.shape[0]
    block = rows // WIDTHS
    row = lax.broadcasted_iota(jnp.int32, (rows, rows), 0)
    column = lax.broadcasted_iota(jnp.int32, (rows, rows), 1)
    sample = (row + place_ref[0] * block) & (rows - 1)
    shard = rows // (WIDTHS * DEPTHS * CORES)
    owner, mine = sample // shard, place_ref[1]
    side = (owner ^ mine) & (CORES - 1)
    depth = (mine // CORES - owner // CORES) & (DEPTHS - 1)
    width = (owner ^ mine) // (DEPTHS * CORES)
    source = ((side * WIDTHS + width) * DEPTHS + depth) * shard + (sample & (shard - 1))
    out_ref[...] = (source == column).astype(F32).astype(BF16)


def choice(place, rows):
    return pl.pallas_call(
        choice_kernel,
        out_shape=jax.ShapeDtypeStruct((rows, rows), BF16),
        in_specs=[pl.BlockSpec(memory_space=pltpu.SMEM)],
        out_specs=whole(),
        compiler_params=params(),
        cost_estimate=pl.CostEstimate(
            flops=20 * rows * rows, transcendentals=0, bytes_accessed=2 * rows * rows
        ),
        name="choice",
    )(place)


def order_kernel(chosen_ref, *refs):
    *sets, out_ref = refs

    @pl.loop(0, out_ref.shape[1] // CAND_TILE)
    def _(tile):
        cols = pl.ds(pl.multiple_of(tile * CAND_TILE, CAND_TILE), CAND_TILE)
        lines = jnp.concatenate([held[:, cols] for held in sets], axis=0)
        out_ref[:, cols] = jnp.dot(
            chosen_ref[...], lines, preferred_element_type=F32
        ).astype(BF16)


def in_order(chosen, sets):
    rows, columns = len(sets) * sets[0].shape[0], sets[0].shape[1]
    return pl.pallas_call(
        order_kernel,
        out_shape=jax.ShapeDtypeStruct((rows, columns), BF16),
        in_specs=[whole()] * (1 + len(sets)),
        out_specs=whole(),
        compiler_params=params(),
        cost_estimate=pl.CostEstimate(
            flops=2 * rows * rows * columns, transcendentals=0, bytes_accessed=4 * rows * columns
        ),
    )(chosen, *sets)


def product_kernel(coef_ref, weight_ref, *refs):
    count = (len(refs) - WIDTHS) // 2
    features, kernels, outs = refs[:count], refs[count : 2 * count], refs[2 * count :]
    block = coef_ref.shape[0] // WIDTHS
    cands = features[0].shape[1]
    for chunk in range(count):
        @pl.loop(0, cands // CAND_TILE)
        def _(tile, chunk=chunk):
            cols = pl.ds(pl.multiple_of(tile * CAND_TILE, CAND_TILE), CAND_TILE)
            total = jnp.dot(coef_ref[...], features[chunk][:, cols], preferred_element_type=F32)
            total = total + jnp.dot(
                weight_ref[...], kernels[chunk][:, cols], preferred_element_type=F32
            )
            place = pl.ds(
                pl.multiple_of(chunk * cands + tile * CAND_TILE, CAND_TILE), CAND_TILE
            )
            for target, out in enumerate(outs):
                rows = slice(target * block, (target + 1) * block)
                out[:, place] = total[rows].astype(out.dtype)


def products(coefs, weights, features, kernels):
    count, cands = len(features), features[0].shape[1]
    block = coefs.shape[0] // WIDTHS
    feats, obs = features[0].shape[0], kernels[0].shape[0]
    shape = (block, count * cands)
    out_shapes = (jax.ShapeDtypeStruct(shape, F32),) + (jax.ShapeDtypeStruct(shape, BF16),) * (
        WIDTHS - 1
    )
    return pl.pallas_call(
        product_kernel,
        out_shape=out_shapes,
        in_specs=[whole()] * (2 + 2 * count),
        out_specs=(whole(),) * WIDTHS,
        compiler_params=params(),
        cost_estimate=pl.CostEstimate(
            flops=2 * coefs.shape[0] * (feats + obs) * count * cands,
            transcendentals=0,
            bytes_accessed=2 * (feats + obs) * count * cands,
        ),
    )(coefs, weights, *features, *kernels)


def exchange_pairs(mask):
    devices = WIDTHS * DEPTHS * CORES
    return [(i, i ^ mask) for i in range(devices)]


def ring_pairs(step):
    line = DEPTHS * CORES
    return [
        (i, i // line * line + (i + step * CORES) % line) for i in range(WIDTHS * line)
    ]


def stack_kernel(*refs):
    *pieces, out_ref, rows = refs
    count = pieces[0].shape[0]
    if count % 16 == 0:
        for index, piece in enumerate(pieces):
            out_ref[index * count : (index + 1) * count, :] = piece[...]
        return
    for index, piece in enumerate(pieces):
        rows[index * count : (index + 1) * count, :] = piece[...].astype(F32)
    out_ref[...] = rows[...].astype(BF16)


def stack(pieces):
    shape = (len(pieces) * pieces[0].shape[0], pieces[0].shape[1])
    return pl.pallas_call(
        stack_kernel,
        out_shape=jax.ShapeDtypeStruct(shape, BF16),
        in_specs=[whole()] * len(pieces),
        out_specs=whole(),
        scratch_shapes=[pltpu.VMEM(shape, F32)],
        compiler_params=params(),
        cost_estimate=pl.CostEstimate(
            flops=0, transcendentals=0, bytes_accessed=4 * shape[0] * shape[1]
        ),
    )(*pieces)


def spread(piece):
    def swap(held, pairs):
        return lax.ppermute(held, "cand", pairs)

    ups, downs = [piece], [piece]
    for hop in range(1, DEPTHS // 2 + 1):
        ups.append(swap(ups[-1], ring_pairs(1)))
        if hop < DEPTHS // 2:
            downs.append(swap(downs[-1], ring_pairs(-1)))
    held = stack(ups + downs[:0:-1])
    others = [swap(held, exchange_pairs(hop * DEPTHS * CORES)) for hop in range(1, WIDTHS)]
    near = stack([held] + others)
    return near, swap(near, exchange_pairs(1))


def split_kernel(inverse_ref, factor_ref, high_ref, middle_ref, low_ref):
    first = pl.program_id(0) == 0
    values = jnp.where(first, inverse_ref[...], factor_ref[...])
    high, middle, low = three_pieces(values)
    high_ref[...] = high.astype(BF16)
    middle_ref[...] = middle.astype(BF16)
    low_ref[...] = low.astype(BF16)


def split(diag_inv, factor_rows, sections):
    block = diag_inv.shape
    columns = sections * block[1]
    return pl.pallas_call(
        split_kernel,
        out_shape=(jax.ShapeDtypeStruct((block[0], columns), BF16),) * 3,
        grid=(sections,),
        in_specs=[
            pl.BlockSpec(block, lambda i: (0, 0)),
            pl.BlockSpec(block, lambda i: (0, jnp.maximum(i - 1, 0))),
        ],
        out_specs=(pl.BlockSpec(block, lambda i: (0, i)),) * 3,
        compiler_params=params(),
        cost_estimate=pl.CostEstimate(
            flops=8 * block[0] * columns, transcendentals=0, bytes_accessed=10 * block[0] * columns
        ),
        name="split",
    )(diag_inv, factor_rows)


def exact_lines(left, lines):
    rows = left.shape[0]
    lines[...] = jnp.zeros_like(lines)
    for index, piece in enumerate(three_pieces(left)):
        lines[index * rows : (index + 1) * rows, :] = piece
    return lines[...].astype(BF16)


def exact_dot(lines, rows, pieces, columns):
    total = None
    for piece, count in zip(pieces[::-1], (1, 2, 3)):
        product = jnp.dot(lines, piece[:, columns], preferred_element_type=F32)
        for index in reversed(range(count)):
            term = product[index * rows : (index + 1) * rows]
            total = term if total is None else total + term
    return total


def solve_kernel(
    section, place_ref, whitened_ref, carried_ref, weights_ref, high_ref, middle_ref, low_ref,
    *rest,
):
    *update_ref, solved_ref, lines = rest
    pieces = (high_ref, middle_ref, low_ref)
    count, width = whitened_ref.shape
    remaining = whitened_ref[...]
    if carried_ref is not None:
        remaining = remaining - carried_ref[:, section * width : (section + 1) * width]
    solved = exact_dot(exact_lines(remaining, lines), count, pieces, slice(0, width))
    wire = solved.astype(BF16)
    if weights_ref is not None:
        wire = jnp.where(place_ref[0] == section, wire.astype(F32), weights_ref[...].astype(F32))
    solved_ref[...] = wire.astype(BF16)
    if section > 0:
        left = exact_lines(solved, lines)

        @pl.loop(0, section)
        def _(earlier):
            first = pl.multiple_of(earlier * width, width)
            later = pl.multiple_of((earlier + 1) * width, width)
            update = exact_dot(left, count, pieces, pl.ds(later, width))
            if carried_ref is not None:
                update = update + carried_ref[:, pl.ds(first, width)]
            update_ref[0][:, pl.ds(first, width)] = update


def solve(section, place, whitened, carried, weights, pieces):
    count, width = whitened.shape
    out_shape = [jax.ShapeDtypeStruct((count, width), BF16)]
    if section > 0:
        out_shape.insert(0, jax.ShapeDtypeStruct((count, section * width), F32))
    columns = (section + 1) * width

    def kernel(place_ref, whitened_ref, *refs):
        if carried is None:
            refs = (None, None) + refs
        solve_kernel(section, place_ref, whitened_ref, *refs)

    held = [] if carried is None else [carried, weights]
    results = pl.pallas_call(
        kernel,
        out_shape=out_shape,
        in_specs=[pl.BlockSpec(memory_space=pltpu.SMEM)] + [whole()] * (1 + len(held) + 3),
        out_specs=[whole()] * len(out_shape),
        scratch_shapes=[pltpu.VMEM((16, width), F32)],
        compiler_params=params(),
        cost_estimate=pl.CostEstimate(
            flops=2 * 36 * width * columns, transcendentals=0, bytes_accessed=6 * width * columns
        ),
    )(place, whitened, *held, *pieces)
    return results if section > 0 else (None, results[0])


def solve_chain(place, whitened, factor_rows, diag_inv):
    sections = lax.axis_size("rows")
    pieces = split(diag_inv, factor_rows, sections)
    carried = weights = None
    for section in reversed(range(sections)):
        carried, weights = solve(section, place, whitened, carried, weights, pieces)
        if section > 0:
            carried = lax.ppermute(carried, "rows", [(section, section - 1)])
    return weights


def body(
    whitened,
    factor_rows,
    diag_inv,
    observed,
    inv_length,
    grid_coords,
    frequencies,
    phases,
    prior_coef,
):
    place = jnp.stack([lax.axis_index("rows"), lax.axis_index("cand")]).astype(jnp.int32)
    chosen = choice(place, whitened.shape[0] * lax.axis_size("cand"))
    coef_sets = spread(prior_coef)
    weights = solve_chain(place, whitened, factor_rows, diag_inv)
    weight_sets = spread(weights)
    turns, exponent, levels = prepare(frequencies, phases, observed, inv_length, grid_coords)
    made = [tiles(turns, exponent, levels, chunk) for chunk in range(CHUNKS)]
    coefs = in_order(chosen, coef_sets)
    solved = in_order(chosen, weight_sets)
    rows = lax.axis_size("rows")
    each = CHUNKS // PARTS
    sums = []
    for part in range(PARTS):
        mine = made[part * each : (part + 1) * each]
        own, *away = products(coefs, solved, [m[0] for m in mine], [m[1] for m in mine])
        total = own
        for shift, block in enumerate(away, 1):
            pairs = [(i, (i + shift) % rows) for i in range(rows)]
            total = total + lax.ppermute(block, "rows", pairs).astype(F32)
        sums.append(total)
    return jnp.concatenate(sums, axis=1).T


def solution(mesh):
    in_specs = (
        P("cand", "rows"),
        P("rows", None),
        P("rows", None),
        P(None, "rows"),
        P(),
        P(None, "cand"),
        P(None, "rows"),
        P("rows"),
        P("cand", "rows"),
    )
    out_specs = P("cand", "rows")

    return jax.shard_map(body, mesh=mesh, in_specs=in_specs, out_specs=out_specs, check_vma=False)
```

```python
import jax
import jax.numpy as jnp
from jax import lax
from jax.experimental import pallas as pl
from jax.experimental.pallas import tpu as pltpu
from jax.sharding import PartitionSpec as P

F32 = jnp.float32
BF16 = jnp.bfloat16
GRID = 21
DIM = 22
CORES = 2
DEPTHS = 8
WIDTHS = 4
LANES = 128
STRIPE = 24
ROW_CHUNK = 256
CAND_TILE = 256
CHUNKS = 8
PARTS = 2
VMEM_BYTES = 16 * 2**20
LOG2E = 1.4426950408889634
INV_TURN = 0.15915494309189535
SINE = (0.55535848, -0.91343016, 0.4493464, -0.09804192)


def params(limit=VMEM_BYTES):
    return pltpu.CompilerParams(vmem_limit_bytes=limit)


def whole():
    return pl.BlockSpec(memory_space=pltpu.VMEM)


def three_pieces(values):
    high = values.astype(BF16).astype(F32)
    rest = values - high
    middle = rest.astype(BF16).astype(F32)
    return high, middle, (rest - middle).astype(BF16).astype(F32)


def stack_pieces(scratch, values, tail):
    scratch[...] = jnp.zeros_like(scratch)
    for piece, part in enumerate(values):
        scratch[piece * STRIPE : piece * STRIPE + DIM, :] = part
    row = lax.broadcasted_iota(jnp.int32, (8, scratch.shape[1]), 0)
    block = jnp.zeros((8, scratch.shape[1]), F32)
    for index, line in enumerate(tail):
        block = jnp.where(row == index, line, block)
    scratch[3 * STRIPE : 3 * STRIPE + 8, :] = block


def prepare_kernel(*refs):
    sources, refs = refs[:7], refs[7:]
    (turns_ref, exponent_ref, levels_ref, inverse_ref, factor_ref), refs = refs[:5], refs[5:]
    (freq_ref, phase_ref, observed_ref, scale_ref, grid_ref), refs = refs[:5], refs[5:]
    wide, narrow, tall, sems = refs
    targets = (freq_ref, phase_ref, observed_ref, scale_ref, grid_ref, inverse_ref, factor_ref)
    copies = [
        pltpu.make_async_copy(
            source.at[:, : target.shape[1]], target, sems.at[index]
        )
        for index, (source, target) in enumerate(zip(sources, targets))
    ]
    for copy in copies:
        copy.start()
    for copy in copies[:5]:
        copy.wait()
    stack_pieces(
        wide,
        three_pieces(freq_ref[...] * (INV_TURN / (GRID - 1))),
        three_pieces(phase_ref[...] * INV_TURN),
    )
    for start in range(0, wide.shape[1], 512):
        turns_ref[start : start + 512, :] = wide[:, start : start + 512].T.astype(BF16)
    scale = jnp.broadcast_to(scale_ref[...], (DIM, DIM))
    line = lax.broadcasted_iota(jnp.int32, (DIM, DIM), 0)
    lane = lax.broadcasted_iota(jnp.int32, (DIM, DIM), 1)
    scale = jnp.sum(jnp.where(line == lane, scale, 0.0), axis=1, keepdims=True)
    squares = scale * scale
    observed = observed_ref[...]
    ones = jnp.ones((1, narrow.shape[1]), F32)
    norm = jnp.sum(observed * observed * squares, axis=0, keepdims=True) * (-0.5 * LOG2E)
    stack_pieces(
        narrow,
        three_pieces(observed * squares * (LOG2E / (GRID - 1))),
        three_pieces(norm) + (ones, ones, ones),
    )
    exponent_ref[...] = narrow[...].T.astype(BF16)
    levels = grid_ref[...].astype(F32)
    ones = jnp.ones((1, tall.shape[1]), F32)
    norm = jnp.sum(levels * levels * squares, axis=0, keepdims=True) * (
        -0.5 * LOG2E / (GRID - 1) ** 2
    )
    stack_pieces(tall, (levels, levels, levels), (ones, ones, ones) + three_pieces(norm))
    levels_ref[...] = tall[...].astype(BF16)
    for copy in copies[5:]:
        copy.wait()


def prepare(frequencies, phases, observed, inv_length, grid_coords, diag_inv, factor_rows):
    feats, obs, cands = frequencies.shape[1], observed.shape[1], grid_coords.shape[1]
    arrays = (frequencies, phases[None, :], observed, inv_length[None, :], grid_coords)
    earlier = factor_rows.shape[1] - diag_inv.shape[1]
    return pl.pallas_call(
        prepare_kernel,
        out_shape=(
            jax.ShapeDtypeStruct((feats, LANES), BF16),
            jax.ShapeDtypeStruct((obs, LANES), BF16),
            jax.ShapeDtypeStruct((LANES, cands), BF16),
            jax.ShapeDtypeStruct(diag_inv.shape, F32),
            jax.ShapeDtypeStruct((factor_rows.shape[0], earlier), F32),
        ),
        in_specs=[pl.BlockSpec(memory_space=pl.ANY)] * 7,
        out_specs=(whole(),) * 5,
        scratch_shapes=[pltpu.VMEM(array.shape, array.dtype) for array in arrays]
        + [
            pltpu.VMEM((LANES, feats), F32),
            pltpu.VMEM((LANES, obs), F32),
            pltpu.VMEM((LANES, cands), F32),
            pltpu.SemaphoreType.DMA((7,)),
        ],
        compiler_params=params(44 * 2**20),
        cost_estimate=pl.CostEstimate(flops=10**7, transcendentals=0, bytes_accessed=8 * 2**20),
        name="prepare",
    )(*arrays, diag_inv, factor_rows)


def cosine(turns):
    near = turns - jnp.round(turns)
    square = near * near
    poly = ((SINE[3] * square + SINE[2]) * square + SINE[1]) * square + SINE[0]
    sine = near * poly
    return (0.015625 - sine * sine).astype(BF16)


def tile_kernel(turns_ref, exponent_ref, levels_ref, features_ref, kernel_ref):
    levels = levels_ref[...]
    for start in range(0, turns_ref.shape[0], ROW_CHUNK):
        rows = slice(start, start + ROW_CHUNK)
        turns = jnp.dot(turns_ref[rows, :], levels, preferred_element_type=F32)
        features_ref[rows, :] = cosine(turns)
    for start in range(0, exponent_ref.shape[0], ROW_CHUNK):
        rows = slice(start, start + ROW_CHUNK)
        exponent = jnp.dot(exponent_ref[rows, :], levels, preferred_element_type=F32)
        kernel_ref[rows, :] = jnp.exp2(exponent).astype(BF16)


def tiles(turns, exponent, levels, chunk):
    feats, obs = turns.shape[0], exponent.shape[0]
    cands = levels.shape[1] // CHUNKS
    steps = cands // CAND_TILE
    return pl.pallas_call(
        tile_kernel,
        out_shape=(
            jax.ShapeDtypeStruct((feats, cands), BF16),
            jax.ShapeDtypeStruct((obs, cands), BF16),
        ),
        grid=(steps,),
        in_specs=[
            whole(),
            whole(),
            pl.BlockSpec((LANES, CAND_TILE), lambda i: (0, i + chunk * steps)),
        ],
        out_specs=(
            pl.BlockSpec((feats, CAND_TILE), lambda i: (0, i)),
            pl.BlockSpec((obs, CAND_TILE), lambda i: (0, i)),
        ),
        compiler_params=params(),
        cost_estimate=pl.CostEstimate(
            flops=24 * (feats + obs) * cands,
            transcendentals=obs * cands,
            bytes_accessed=2 * (feats + obs) * cands,
        ),
    )(turns, exponent, levels)


def order_kernel(near_ref, far_ref, out_ref):
    rows, half = out_ref.shape[0], near_ref.shape[0] // WIDTHS
    block = rows // WIDTHS
    shard = rows // (WIDTHS * DEPTHS * CORES)
    across, mine = lax.axis_index("rows"), lax.axis_index("cand")
    row = lax.broadcasted_iota(jnp.int32, (block, block), 0)
    column = lax.broadcasted_iota(jnp.int32, (block, block), 1)
    offset = (row // shard) ^ (mine & (DEPTHS * CORES - 1))
    source = ((offset & (CORES - 1)) * DEPTHS + offset // CORES) * shard + (row & (shard - 1))
    chosen = (source == column).astype(F32).astype(BF16)
    for target in range(WIDTHS):
        width = ((across + target) & (WIDTHS - 1)) ^ (mine // (DEPTHS * CORES))
        held = pl.ds(pl.multiple_of(width * half, half), half)
        lines = jnp.concatenate([near_ref[held, :], far_ref[held, :]], axis=0)
        out_ref[target * block : (target + 1) * block, :] = jnp.dot(
            chosen, lines, preferred_element_type=F32
        ).astype(BF16)


def in_order(near, far):
    rows, columns = 2 * near.shape[0], near.shape[1]
    return pl.pallas_call(
        order_kernel,
        out_shape=jax.ShapeDtypeStruct((rows, columns), BF16),
        in_specs=[whole(), whole()],
        out_specs=whole(),
        compiler_params=params(),
        cost_estimate=pl.CostEstimate(
            flops=2 * rows * rows * columns, transcendentals=0, bytes_accessed=4 * rows * columns
        ),
    )(near, far)


def prior_kernel(coef_ref, *refs):
    *features, out_ref = refs
    cands = features[0].shape[1]
    for chunk, feature_ref in enumerate(features):
        out_ref[:, chunk * cands : (chunk + 1) * cands] = jnp.dot(
            coef_ref[...], feature_ref[...], preferred_element_type=F32
        )


def cross_kernel(weight_ref, prior_ref, *refs):
    kernels, outs = refs[:-WIDTHS], refs[-WIDTHS:]
    block = weight_ref.shape[0] // WIDTHS
    cands = kernels[0].shape[1]
    for chunk, kernel_ref in enumerate(kernels):
        cols = slice(chunk * cands, (chunk + 1) * cands)
        total = prior_ref[:, cols] + jnp.dot(
            weight_ref[...], kernel_ref[...], preferred_element_type=F32
        )
        for target, out in enumerate(outs):
            rows = slice(target * block, (target + 1) * block)
            out[:, cols] = total[rows].astype(out.dtype)


def prior_product(coefs, features):
    rows, cands = coefs.shape[0], len(features) * features[0].shape[1]
    feats = coefs.shape[1]
    return pl.pallas_call(
        prior_kernel,
        out_shape=jax.ShapeDtypeStruct((rows, cands), F32),
        in_specs=[whole()] * (1 + len(features)),
        out_specs=whole(),
        compiler_params=params(),
        cost_estimate=pl.CostEstimate(
            flops=2 * rows * feats * cands, transcendentals=0, bytes_accessed=2 * feats * cands
        ),
    )(coefs, *features)


def cross_product(weights, prior, kernels):
    rows, cands = prior.shape
    obs = weights.shape[1]
    shape = (rows // WIDTHS, cands)
    out_shapes = (jax.ShapeDtypeStruct(shape, F32),) + (jax.ShapeDtypeStruct(shape, BF16),) * (
        WIDTHS - 1
    )
    return pl.pallas_call(
        cross_kernel,
        out_shape=out_shapes,
        in_specs=[whole()] * (2 + len(kernels)),
        out_specs=(whole(),) * WIDTHS,
        compiler_params=params(),
        cost_estimate=pl.CostEstimate(
            flops=2 * rows * obs * cands, transcendentals=0, bytes_accessed=8 * rows * cands
        ),
    )(weights, prior, *kernels)


def total_kernel(*refs):
    *parts, out_ref = refs
    cands = parts[0].shape[1]
    for part in range(len(parts) // WIDTHS):
        own, *others = parts[part * WIDTHS : (part + 1) * WIDTHS]
        total = own[...]
        for other in others:
            total = total + other[...].astype(F32)
        out_ref[:, part * cands : (part + 1) * cands] = total


def total(parts):
    flat = [block for part in parts for block in part]
    shape = (flat[0].shape[0], len(parts) * flat[0].shape[1])
    return pl.pallas_call(
        total_kernel,
        out_shape=jax.ShapeDtypeStruct(shape, F32),
        in_specs=[whole()] * len(flat),
        out_specs=whole(),
        compiler_params=params(),
        cost_estimate=pl.CostEstimate(
            flops=3 * shape[0] * shape[1], transcendentals=0, bytes_accessed=14 * shape[0] * shape[1]
        ),
        name="total",
    )(*flat)


def exchange_pairs(mask):
    devices = WIDTHS * DEPTHS * CORES
    return [(i, i ^ mask) for i in range(devices)]


def stack_kernel(*refs):
    *pieces, out_ref, rows = refs
    count = pieces[0].shape[0]
    if count % 16 == 0:
        for index, piece in enumerate(pieces):
            out_ref[index * count : (index + 1) * count, :] = piece[...]
        return
    for index, piece in enumerate(pieces):
        rows[index * count : (index + 1) * count, :] = piece[...].astype(F32)
    out_ref[...] = rows[...].astype(BF16)


def stack(pieces):
    shape = (len(pieces) * pieces[0].shape[0], pieces[0].shape[1])
    return pl.pallas_call(
        stack_kernel,
        out_shape=jax.ShapeDtypeStruct(shape, BF16),
        in_specs=[whole()] * len(pieces),
        out_specs=whole(),
        scratch_shapes=[pltpu.VMEM(shape, F32)],
        compiler_params=params(),
        cost_estimate=pl.CostEstimate(
            flops=0, transcendentals=0, bytes_accessed=4 * shape[0] * shape[1]
        ),
    )(*pieces)


def spread(piece, at_once):
    def swap(held, pairs):
        return lax.ppermute(held, "cand", pairs)

    held = piece
    for hop in (1, 2, 4):
        other = swap(held, exchange_pairs(hop * CORES))
        held = stack([held, other])
    step = DEPTHS * CORES
    if at_once:
        others = [swap(held, exchange_pairs(hop * step)) for hop in range(1, WIDTHS)]
        near = stack([held] + others)
    else:
        near = stack([held, swap(held, exchange_pairs(step))])
        near = stack([near, swap(near, exchange_pairs(2 * step))])
    return near, swap(near, exchange_pairs(1))


def exact_lines(left, lines):
    rows = left.shape[0]
    lines[...] = jnp.zeros_like(lines)
    for index, piece in enumerate(three_pieces(left)):
        lines[index * rows : (index + 1) * rows, :] = piece
    return lines[...].astype(BF16)


def exact_dot(lines, rows, right):
    total = None
    for piece, count in zip(three_pieces(right)[::-1], (1, 2, 3)):
        product = jnp.dot(lines, piece.astype(BF16), preferred_element_type=F32)
        for index in reversed(range(count)):
            term = product[index * rows : (index + 1) * rows]
            total = term if total is None else total + term
    return total


def solve_kernel(
    section, whitened_ref, inverse_ref, factor_ref, carried_ref, weights_ref, *rest
):
    *update_ref, solved_ref, lines = rest
    count, width = whitened_ref.shape
    active = lax.axis_index("rows") == section

    @pl.when(active)
    def _():
        remaining = whitened_ref[...]
        if carried_ref is not None:
            remaining = remaining - carried_ref[:, section * width : (section + 1) * width]
        solved = exact_dot(exact_lines(remaining, lines), count, inverse_ref[...])
        solved_ref[...] = solved.astype(BF16)
        if section > 0:
            left = exact_lines(solved, lines)

            @pl.loop(0, section)
            def _(earlier):
                cols = pl.ds(pl.multiple_of(earlier * width, width), width)
                update = exact_dot(left, count, factor_ref[:, cols])
                if carried_ref is not None:
                    update = update + carried_ref[:, cols]
                update_ref[0][:, cols] = update

    if weights_ref is not None:
        @pl.when(jnp.logical_not(active))
        def _():
            solved_ref[...] = weights_ref[...]


def solve(section, whitened, carried, weights, diag_inv, factor_rows):
    count, width = whitened.shape
    out_shape = [jax.ShapeDtypeStruct((count, width), BF16)]
    if section > 0:
        out_shape.insert(0, jax.ShapeDtypeStruct((count, section * width), F32))
    first = carried is None

    def kernel(whitened_ref, inverse_ref, factor_ref, *refs):
        if first:
            refs = (None, None) + refs
        solve_kernel(section, whitened_ref, inverse_ref, factor_ref, *refs)

    held = [] if first else [carried, weights]
    columns = (section + 1) * width
    results = pl.pallas_call(
        kernel,
        out_shape=out_shape,
        in_specs=[whole()] * (3 + len(held)),
        out_specs=[whole()] * len(out_shape),
        scratch_shapes=[pltpu.VMEM((16, width), F32)],
        compiler_params=params(),
        cost_estimate=pl.CostEstimate(
            flops=2 * 36 * width * columns, transcendentals=0, bytes_accessed=4 * width * columns
        ),
    )(whitened, diag_inv, factor_rows, *held)
    return results if section > 0 else (None, results[0])


def solve_chain(whitened, factor_rows, diag_inv):
    sections = lax.axis_size("rows")
    carried = weights = None
    for section in reversed(range(sections)):
        carried, weights = solve(section, whitened, carried, weights, diag_inv, factor_rows)
        if section > 0:
            carried = lax.ppermute(carried, "rows", [(section, section - 1)])
    return weights


def body(
    whitened,
    factor_rows,
    diag_inv,
    observed,
    inv_length,
    grid_coords,
    frequencies,
    phases,
    prior_coef,
):
    turns, exponent, levels, inverse, factor = prepare(
        frequencies, phases, observed, inv_length, grid_coords, diag_inv, factor_rows
    )
    coef_near, coef_far = spread(prior_coef, False)
    weights = solve_chain(whitened, factor, inverse)
    weight_near, weight_far = spread(weights, True)
    made = [tiles(turns, exponent, levels, chunk) for chunk in range(CHUNKS)]
    coefs = in_order(coef_near, coef_far)
    solved = in_order(weight_near, weight_far)
    rows = lax.axis_size("rows")
    each = CHUNKS // PARTS
    parts = []
    for part in range(PARTS):
        mine = made[part * each : (part + 1) * each]
        prior = prior_product(coefs, [m[0] for m in mine])
        own, *away = cross_product(solved, prior, [m[1] for m in mine])
        arrived = []
        for shift, block in enumerate(away, 1):
            pairs = [(i, (i + shift) % rows) for i in range(rows)]
            arrived.append(lax.ppermute(block, "rows", pairs))
        parts.append([own] + arrived)
    return total(parts).T


def solution(mesh):
    in_specs = (
        P("cand", "rows"),
        P("rows", None),
        P("rows", None),
        P(None, "rows"),
        P(),
        P(None, "cand"),
        P(None, "rows"),
        P("rows"),
        P("cand", "rows"),
    )
    out_specs = P("cand", "rows")

    return jax.shard_map(body, mesh=mesh, in_specs=in_specs, out_specs=out_specs, check_vma=False)
```

```python
import jax
import jax.numpy as jnp
from jax import lax
from jax.experimental import pallas as pl
from jax.experimental.pallas import tpu as pltpu
from jax.sharding import PartitionSpec as P

F32 = jnp.float32
BF16 = jnp.bfloat16
GRID = 21
DIM = 22
CORES = 2
DEPTHS = 8
WIDTHS = 4
LANES = 128
STRIPE = 24
ROW_CHUNK = 256
CAND_TILE = 256
CHUNKS = 8
PARTS = 2
VMEM_BYTES = 16 * 2**20
LOG2E = 1.4426950408889634
INV_TURN = 0.15915494309189535
SINE = (0.55535848, -0.91343016, 0.4493464, -0.09804192)


def params(limit=VMEM_BYTES):
    return pltpu.CompilerParams(vmem_limit_bytes=limit)


def whole():
    return pl.BlockSpec(memory_space=pltpu.VMEM)


def three_pieces(values):
    high = values.astype(BF16).astype(F32)
    rest = values - high
    middle = rest.astype(BF16).astype(F32)
    return high, middle, (rest - middle).astype(BF16).astype(F32)


def stack_pieces(scratch, values, tail):
    scratch[...] = jnp.zeros_like(scratch)
    for piece, part in enumerate(values):
        scratch[piece * STRIPE : piece * STRIPE + DIM, :] = part
    row = lax.broadcasted_iota(jnp.int32, (8, scratch.shape[1]), 0)
    block = jnp.zeros((8, scratch.shape[1]), F32)
    for index, line in enumerate(tail):
        block = jnp.where(row == index, line, block)
    scratch[3 * STRIPE : 3 * STRIPE + 8, :] = block


def prepare_kernel(*refs):
    sources, refs = refs[:7], refs[7:]
    (turns_ref, exponent_ref, levels_ref, inverse_ref, factor_ref), refs = refs[:5], refs[5:]
    (freq_ref, phase_ref, observed_ref, scale_ref, grid_ref), refs = refs[:5], refs[5:]
    wide, narrow, tall, sems = refs
    targets = (freq_ref, phase_ref, observed_ref, scale_ref, grid_ref, inverse_ref, factor_ref)
    copies = [
        pltpu.make_async_copy(
            source.at[:, : target.shape[1]], target, sems.at[index]
        )
        for index, (source, target) in enumerate(zip(sources, targets))
    ]
    for copy in copies:
        copy.start()
    for copy in copies[:5]:
        copy.wait()
    stack_pieces(
        wide,
        three_pieces(freq_ref[...] * (INV_TURN / (GRID - 1))),
        three_pieces(phase_ref[...] * INV_TURN),
    )
    for start in range(0, wide.shape[1], 512):
        turns_ref[start : start + 512, :] = wide[:, start : start + 512].T.astype(BF16)
    scale = jnp.broadcast_to(scale_ref[...], (DIM, DIM))
    line = lax.broadcasted_iota(jnp.int32, (DIM, DIM), 0)
    lane = lax.broadcasted_iota(jnp.int32, (DIM, DIM), 1)
    scale = jnp.sum(jnp.where(line == lane, scale, 0.0), axis=1, keepdims=True)
    squares = scale * scale
    observed = observed_ref[...]
    ones = jnp.ones((1, narrow.shape[1]), F32)
    norm = jnp.sum(observed * observed * squares, axis=0, keepdims=True) * (-0.5 * LOG2E)
    stack_pieces(
        narrow,
        three_pieces(observed * squares * (LOG2E / (GRID - 1))),
        three_pieces(norm) + (ones, ones, ones),
    )
    exponent_ref[...] = narrow[...].T.astype(BF16)
    levels = grid_ref[...].astype(F32)
    ones = jnp.ones((1, tall.shape[1]), F32)
    norm = jnp.sum(levels * levels * squares, axis=0, keepdims=True) * (
        -0.5 * LOG2E / (GRID - 1) ** 2
    )
    stack_pieces(tall, (levels, levels, levels), (ones, ones, ones) + three_pieces(norm))
    levels_ref[...] = tall[...].astype(BF16)
    for copy in copies[5:]:
        copy.wait()


def prepare(frequencies, phases, observed, inv_length, grid_coords, diag_inv, factor_rows):
    feats, obs, cands = frequencies.shape[1], observed.shape[1], grid_coords.shape[1]
    arrays = (frequencies, phases[None, :], observed, inv_length[None, :], grid_coords)
    earlier = factor_rows.shape[1] - diag_inv.shape[1]
    return pl.pallas_call(
        prepare_kernel,
        out_shape=(
            jax.ShapeDtypeStruct((feats, LANES), BF16),
            jax.ShapeDtypeStruct((obs, LANES), BF16),
            jax.ShapeDtypeStruct((LANES, cands), BF16),
            jax.ShapeDtypeStruct(diag_inv.shape, F32),
            jax.ShapeDtypeStruct((factor_rows.shape[0], earlier), F32),
        ),
        in_specs=[pl.BlockSpec(memory_space=pl.ANY)] * 7,
        out_specs=(whole(),) * 5,
        scratch_shapes=[pltpu.VMEM(array.shape, array.dtype) for array in arrays]
        + [
            pltpu.VMEM((LANES, feats), F32),
            pltpu.VMEM((LANES, obs), F32),
            pltpu.VMEM((LANES, cands), F32),
            pltpu.SemaphoreType.DMA((7,)),
        ],
        compiler_params=params(),
        cost_estimate=pl.CostEstimate(flops=10**7, transcendentals=0, bytes_accessed=8 * 2**20),
        name="prepare",
    )(
        *(
            pltpu.with_memory_space_constraint(array, pltpu.HBM)
            for array in (*arrays, diag_inv, factor_rows)
        )
    )


def cosine(turns):
    near = turns - jnp.round(turns)
    square = near * near
    poly = ((SINE[3] * square + SINE[2]) * square + SINE[1]) * square + SINE[0]
    sine = near * poly
    return (0.015625 - sine * sine).astype(BF16)


def tile_kernel(turns_ref, exponent_ref, levels_ref, features_ref, kernel_ref):
    levels = levels_ref[...]
    for start in range(0, turns_ref.shape[0], ROW_CHUNK):
        rows = slice(start, start + ROW_CHUNK)
        turns = jnp.dot(turns_ref[rows, :], levels, preferred_element_type=F32)
        features_ref[rows, :] = cosine(turns)
    for start in range(0, exponent_ref.shape[0], ROW_CHUNK):
        rows = slice(start, start + ROW_CHUNK)
        exponent = jnp.dot(exponent_ref[rows, :], levels, preferred_element_type=F32)
        kernel_ref[rows, :] = jnp.exp2(exponent).astype(BF16)


def tiles(turns, exponent, levels, chunk):
    feats, obs = turns.shape[0], exponent.shape[0]
    cands = levels.shape[1] // CHUNKS
    steps = cands // CAND_TILE
    return pl.pallas_call(
        tile_kernel,
        out_shape=(
            jax.ShapeDtypeStruct((feats, cands), BF16),
            jax.ShapeDtypeStruct((obs, cands), BF16),
        ),
        grid=(steps,),
        in_specs=[
            whole(),
            whole(),
            pl.BlockSpec((LANES, CAND_TILE), lambda i: (0, i + chunk * steps)),
        ],
        out_specs=(
            pl.BlockSpec((feats, CAND_TILE), lambda i: (0, i)),
            pl.BlockSpec((obs, CAND_TILE), lambda i: (0, i)),
        ),
        compiler_params=params(),
        cost_estimate=pl.CostEstimate(
            flops=24 * (feats + obs) * cands,
            transcendentals=obs * cands,
            bytes_accessed=2 * (feats + obs) * cands,
        ),
    )(turns, exponent, levels)


def order_kernel(near_ref, far_ref, out_ref):
    rows, half = out_ref.shape[0], near_ref.shape[0] // WIDTHS
    block = rows // WIDTHS
    shard = rows // (WIDTHS * DEPTHS * CORES)
    across, mine = lax.axis_index("rows"), lax.axis_index("cand")
    row = lax.broadcasted_iota(jnp.int32, (block, block), 0)
    column = lax.broadcasted_iota(jnp.int32, (block, block), 1)
    offset = (row // shard) ^ (mine & (DEPTHS * CORES - 1))
    depth = offset // CORES
    depth = jnp.where(depth < DEPTHS // 2, depth, depth ^ (DEPTHS // 2 - 1))
    source = ((offset & (CORES - 1)) * DEPTHS + depth) * shard + (row & (shard - 1))
    chosen = (source == column).astype(F32).astype(BF16)
    for target in range(WIDTHS):
        width = ((across + target) & (WIDTHS - 1)) ^ (mine // (DEPTHS * CORES))
        width = width ^ (width // 2)
        held = pl.ds(pl.multiple_of(width * half, half), half)
        lines = jnp.concatenate([near_ref[held, :], far_ref[held, :]], axis=0)
        out_ref[target * block : (target + 1) * block, :] = jnp.dot(
            chosen, lines, preferred_element_type=F32
        ).astype(BF16)


def in_order(near, far):
    rows, columns = 2 * near.shape[0], near.shape[1]
    return pl.pallas_call(
        order_kernel,
        out_shape=jax.ShapeDtypeStruct((rows, columns), BF16),
        in_specs=[whole(), whole()],
        out_specs=whole(),
        compiler_params=params(),
        cost_estimate=pl.CostEstimate(
            flops=2 * rows * rows * columns, transcendentals=0, bytes_accessed=4 * rows * columns
        ),
    )(near, far)


def prior_kernel(coef_ref, *refs):
    *features, out_ref = refs
    cands = features[0].shape[1]
    for chunk, feature_ref in enumerate(features):
        out_ref[:, chunk * cands : (chunk + 1) * cands] = jnp.dot(
            coef_ref[...], feature_ref[...], preferred_element_type=F32
        )


def cross_kernel(weight_ref, prior_ref, *refs):
    kernels, outs = refs[:-WIDTHS], refs[-WIDTHS:]
    block = weight_ref.shape[0] // WIDTHS
    cands = kernels[0].shape[1]
    for chunk, kernel_ref in enumerate(kernels):
        cols = slice(chunk * cands, (chunk + 1) * cands)
        total = prior_ref[:, cols] + jnp.dot(
            weight_ref[...], kernel_ref[...], preferred_element_type=F32
        )
        for target, out in enumerate(outs):
            rows = slice(target * block, (target + 1) * block)
            out[:, cols] = total[rows].astype(out.dtype)


def prior_product(coefs, features):
    rows, cands = coefs.shape[0], len(features) * features[0].shape[1]
    feats = coefs.shape[1]
    return pl.pallas_call(
        prior_kernel,
        out_shape=jax.ShapeDtypeStruct((rows, cands), F32),
        in_specs=[whole()] * (1 + len(features)),
        out_specs=whole(),
        compiler_params=params(),
        cost_estimate=pl.CostEstimate(
            flops=2 * rows * feats * cands, transcendentals=0, bytes_accessed=2 * feats * cands
        ),
    )(coefs, *features)


def cross_product(weights, prior, kernels):
    rows, cands = prior.shape
    obs = weights.shape[1]
    shape = (rows // WIDTHS, cands)
    out_shapes = (jax.ShapeDtypeStruct(shape, F32),) + (jax.ShapeDtypeStruct(shape, BF16),) * (
        WIDTHS - 1
    )
    return pl.pallas_call(
        cross_kernel,
        out_shape=out_shapes,
        in_specs=[whole()] * (2 + len(kernels)),
        out_specs=(whole(),) * WIDTHS,
        compiler_params=params(),
        cost_estimate=pl.CostEstimate(
            flops=2 * rows * obs * cands, transcendentals=0, bytes_accessed=8 * rows * cands
        ),
    )(weights, prior, *kernels)


def total_kernel(*refs):
    *parts, out_ref = refs
    cands = parts[0].shape[1]
    for part in range(len(parts) // WIDTHS):
        own, *others = parts[part * WIDTHS : (part + 1) * WIDTHS]
        total = own[...]
        for other in others:
            total = total + other[...].astype(F32)
        out_ref[:, part * cands : (part + 1) * cands] = total


def total(parts):
    flat = [block for part in parts for block in part]
    shape = (flat[0].shape[0], len(parts) * flat[0].shape[1])
    return pl.pallas_call(
        total_kernel,
        out_shape=jax.ShapeDtypeStruct(shape, F32),
        in_specs=[whole()] * len(flat),
        out_specs=whole(),
        compiler_params=params(),
        cost_estimate=pl.CostEstimate(
            flops=3 * shape[0] * shape[1], transcendentals=0, bytes_accessed=14 * shape[0] * shape[1]
        ),
        name="total",
    )(*flat)


def exchange_pairs(mask):
    devices = WIDTHS * DEPTHS * CORES
    return [(i, i ^ mask) for i in range(devices)]


def stack_kernel(*refs):
    *pieces, out_ref, rows = refs
    count = pieces[0].shape[0]
    if count % 16 == 0:
        for index, piece in enumerate(pieces):
            out_ref[index * count : (index + 1) * count, :] = piece[...]
        return
    for index, piece in enumerate(pieces):
        rows[index * count : (index + 1) * count, :] = piece[...].astype(F32)
    out_ref[...] = rows[...].astype(BF16)


def stack(pieces):
    shape = (len(pieces) * pieces[0].shape[0], pieces[0].shape[1])
    return pl.pallas_call(
        stack_kernel,
        out_shape=jax.ShapeDtypeStruct(shape, BF16),
        in_specs=[whole()] * len(pieces),
        out_specs=whole(),
        scratch_shapes=[pltpu.VMEM(shape, F32)],
        compiler_params=params(),
        cost_estimate=pl.CostEstimate(
            flops=0, transcendentals=0, bytes_accessed=4 * shape[0] * shape[1]
        ),
    )(*pieces)


def spread(piece, at_once):
    def swap(held, pairs):
        return lax.ppermute(held, "cand", pairs)

    held = piece
    for hop in (1, 2, 7):
        other = swap(held, exchange_pairs(hop * CORES))
        held = stack([held, other])
    step = DEPTHS * CORES
    if at_once:
        others = [swap(held, exchange_pairs(hop * step)) for hop in (1, 3, 2)]
        near = stack([held] + others)
    else:
        near = stack([held, swap(held, exchange_pairs(step))])
        near = stack([near, swap(near, exchange_pairs(3 * step))])
    return near, swap(near, exchange_pairs(1))


def exact_lines(left, lines):
    rows = left.shape[0]
    lines[...] = jnp.zeros_like(lines)
    for index, piece in enumerate(three_pieces(left)):
        lines[index * rows : (index + 1) * rows, :] = piece
    return lines[...].astype(BF16)


def exact_dot(lines, rows, right):
    total = None
    for piece, count in zip(three_pieces(right)[::-1], (1, 2, 3)):
        product = jnp.dot(lines, piece.astype(BF16), preferred_element_type=F32)
        for index in reversed(range(count)):
            term = product[index * rows : (index + 1) * rows]
            total = term if total is None else total + term
    return total


def solve_kernel(
    section, whitened_ref, inverse_ref, factor_ref, carried_ref, weights_ref, *rest
):
    *update_ref, solved_ref, lines = rest
    count, width = whitened_ref.shape
    active = lax.axis_index("rows") == section

    @pl.when(active)
    def _():
        remaining = whitened_ref[...]
        if carried_ref is not None:
            remaining = remaining - carried_ref[:, section * width : (section + 1) * width]
        solved = exact_dot(exact_lines(remaining, lines), count, inverse_ref[...])
        solved_ref[...] = solved.astype(BF16)
        if section > 0:
            left = exact_lines(solved, lines)

            @pl.loop(0, section)
            def _(earlier):
                cols = pl.ds(pl.multiple_of(earlier * width, width), width)
                update = exact_dot(left, count, factor_ref[:, cols])
                if carried_ref is not None:
                    update = update + carried_ref[:, cols]
                update_ref[0][:, cols] = update

    if weights_ref is not None:
        @pl.when(jnp.logical_not(active))
        def _():
            solved_ref[...] = weights_ref[...]


def solve(section, whitened, carried, weights, diag_inv, factor_rows):
    count, width = whitened.shape
    out_shape = [jax.ShapeDtypeStruct((count, width), BF16)]
    if section > 0:
        out_shape.insert(0, jax.ShapeDtypeStruct((count, section * width), F32))
    first = carried is None

    def kernel(whitened_ref, inverse_ref, factor_ref, *refs):
        if first:
            refs = (None, None) + refs
        solve_kernel(section, whitened_ref, inverse_ref, factor_ref, *refs)

    held = [] if first else [carried, weights]
    columns = (section + 1) * width
    results = pl.pallas_call(
        kernel,
        out_shape=out_shape,
        in_specs=[whole()] * (3 + len(held)),
        out_specs=[whole()] * len(out_shape),
        scratch_shapes=[pltpu.VMEM((16, width), F32)],
        compiler_params=params(),
        cost_estimate=pl.CostEstimate(
            flops=2 * 36 * width * columns, transcendentals=0, bytes_accessed=4 * width * columns
        ),
    )(whitened, diag_inv, factor_rows, *held)
    return results if section > 0 else (None, results[0])


def solve_chain(whitened, factor_rows, diag_inv):
    sections = lax.axis_size("rows")
    carried = weights = None
    for section in reversed(range(sections)):
        carried, weights = solve(section, whitened, carried, weights, diag_inv, factor_rows)
        if section > 0:
            carried = lax.ppermute(carried, "rows", [(section, section - 1)])
    return weights


def body(
    whitened,
    factor_rows,
    diag_inv,
    observed,
    inv_length,
    grid_coords,
    frequencies,
    phases,
    prior_coef,
):
    turns, exponent, levels, inverse, factor = prepare(
        frequencies, phases, observed, inv_length, grid_coords, diag_inv, factor_rows
    )
    coef_near, coef_far = spread(prior_coef, False)
    weights = solve_chain(whitened, factor, inverse)
    weight_near, weight_far = spread(weights, True)
    made = [tiles(turns, exponent, levels, chunk) for chunk in range(CHUNKS)]
    coefs = in_order(coef_near, coef_far)
    solved = in_order(weight_near, weight_far)
    rows = lax.axis_size("rows")
    each = CHUNKS // PARTS
    parts = []
    for part in range(PARTS):
        mine = made[part * each : (part + 1) * each]
        prior = prior_product(coefs, [m[0] for m in mine])
        own, *away = cross_product(solved, prior, [m[1] for m in mine])
        arrived = []
        for shift, block in enumerate(away, 1):
            pairs = [(i, (i + shift) % rows) for i in range(rows)]
            arrived.append(lax.ppermute(block, "rows", pairs))
        parts.append([own] + arrived)
    return total(parts).T


def solution(mesh):
    in_specs = (
        P("cand", "rows"),
        P("rows", None),
        P("rows", None),
        P(None, "rows"),
        P(),
        P(None, "cand"),
        P(None, "rows"),
        P("rows"),
        P("cand", "rows"),
    )
    out_specs = P("cand", "rows")

    return jax.shard_map(body, mesh=mesh, in_specs=in_specs, out_specs=out_specs, check_vma=False)
```

```python
import functools

import jax
import jax.numpy as jnp
from jax import lax
from jax.experimental import pallas as pl
from jax.experimental.pallas import tpu as pltpu
from jax.sharding import PartitionSpec as P

F32 = jnp.float32
BF16 = jnp.bfloat16
GRID = 21
DIM = 22
CORES = 2
DEPTHS = 8
WIDTHS = 4
LANES = 128
STRIPE = 24
ROW_CHUNK = 256
CAND_TILE = 256
CHUNKS = 8
PARTS = ((0, 6), (6, 8))
VMEM_BYTES = 16 * 2**20
LOG2E = 1.4426950408889634
INV_TURN = 0.15915494309189535
SINE = (0.55535848, -0.91343016, 0.4493464, -0.09804192)


def params(limit=VMEM_BYTES):
    return pltpu.CompilerParams(vmem_limit_bytes=limit)


def whole():
    return pl.BlockSpec(memory_space=pltpu.VMEM)


def three_pieces(values):
    high = values.astype(BF16).astype(F32)
    rest = values - high
    middle = rest.astype(BF16).astype(F32)
    return high, middle, (rest - middle).astype(BF16).astype(F32)


def stack_pieces(scratch, values, tail):
    scratch[...] = jnp.zeros_like(scratch)
    for piece, part in enumerate(values):
        scratch[piece * STRIPE : piece * STRIPE + DIM, :] = part
    row = lax.broadcasted_iota(jnp.int32, (8, scratch.shape[1]), 0)
    block = jnp.zeros((8, scratch.shape[1]), F32)
    for index, line in enumerate(tail):
        block = jnp.where(row == index, line, block)
    scratch[3 * STRIPE : 3 * STRIPE + 8, :] = block


def prepare_kernel(*refs):
    sources, refs = refs[:7], refs[7:]
    (turns_ref, exponent_ref, levels_ref, inverse_ref, factor_ref), refs = refs[:5], refs[5:]
    (freq_ref, phase_ref, observed_ref, scale_ref, grid_ref), refs = refs[:5], refs[5:]
    wide, narrow, tall, sems = refs
    targets = (freq_ref, phase_ref, observed_ref, scale_ref, grid_ref, inverse_ref, factor_ref)
    copies = [
        pltpu.make_async_copy(
            source.at[:, : target.shape[1]], target, sems.at[index]
        )
        for index, (source, target) in enumerate(zip(sources, targets))
    ]
    for copy in copies:
        copy.start()
    for copy in copies[:5]:
        copy.wait()
    stack_pieces(
        wide,
        three_pieces(freq_ref[...] * (INV_TURN / (GRID - 1))),
        three_pieces(phase_ref[...] * INV_TURN),
    )
    for start in range(0, wide.shape[1], 512):
        turns_ref[start : start + 512, :] = wide[:, start : start + 512].T.astype(BF16)
    scale = jnp.broadcast_to(scale_ref[...], (DIM, DIM))
    line = lax.broadcasted_iota(jnp.int32, (DIM, DIM), 0)
    lane = lax.broadcasted_iota(jnp.int32, (DIM, DIM), 1)
    scale = jnp.sum(jnp.where(line == lane, scale, 0.0), axis=1, keepdims=True)
    squares = scale * scale
    observed = observed_ref[...]
    ones = jnp.ones((1, narrow.shape[1]), F32)
    norm = jnp.sum(observed * observed * squares, axis=0, keepdims=True) * (-0.5 * LOG2E)
    stack_pieces(
        narrow,
        three_pieces(observed * squares * (LOG2E / (GRID - 1))),
        three_pieces(norm) + (ones, ones, ones),
    )
    exponent_ref[...] = narrow[...].T.astype(BF16)
    levels = grid_ref[...].astype(F32)
    ones = jnp.ones((1, tall.shape[1]), F32)
    norm = jnp.sum(levels * levels * squares, axis=0, keepdims=True) * (
        -0.5 * LOG2E / (GRID - 1) ** 2
    )
    stack_pieces(tall, (levels, levels, levels), (ones, ones, ones) + three_pieces(norm))
    levels_ref[...] = tall[...].astype(BF16)
    for copy in copies[5:]:
        copy.wait()


def prepare(frequencies, phases, observed, inv_length, grid_coords, diag_inv, factor_rows):
    feats, obs, cands = frequencies.shape[1], observed.shape[1], grid_coords.shape[1]
    arrays = (frequencies, phases[None, :], observed, inv_length[None, :], grid_coords)
    earlier = factor_rows.shape[1] - diag_inv.shape[1]
    return pl.pallas_call(
        prepare_kernel,
        out_shape=(
            jax.ShapeDtypeStruct((feats, LANES), BF16),
            jax.ShapeDtypeStruct((obs, LANES), BF16),
            jax.ShapeDtypeStruct((LANES, cands), BF16),
            jax.ShapeDtypeStruct(diag_inv.shape, F32),
            jax.ShapeDtypeStruct((factor_rows.shape[0], earlier), F32),
        ),
        in_specs=[pl.BlockSpec(memory_space=pl.ANY)] * 7,
        out_specs=(whole(),) * 5,
        scratch_shapes=[pltpu.VMEM(array.shape, array.dtype) for array in arrays]
        + [
            pltpu.VMEM((LANES, feats), F32),
            pltpu.VMEM((LANES, obs), F32),
            pltpu.VMEM((LANES, cands), F32),
            pltpu.SemaphoreType.DMA((7,)),
        ],
        compiler_params=params(),
        cost_estimate=pl.CostEstimate(flops=10**7, transcendentals=0, bytes_accessed=8 * 2**20),
        name="prepare",
    )(
        *(
            pltpu.with_memory_space_constraint(array, pltpu.HBM)
            for array in (*arrays, diag_inv, factor_rows)
        )
    )


def cosine(turns):
    near = turns - jnp.round(turns)
    square = near * near
    poly = ((SINE[3] * square + SINE[2]) * square + SINE[1]) * square + SINE[0]
    sine = near * poly
    return (0.015625 - sine * sine).astype(BF16)


def tile_kernel(turns_ref, exponent_ref, levels_ref, features_ref, kernel_ref):
    levels = levels_ref[...]
    for start in range(0, turns_ref.shape[0], ROW_CHUNK):
        rows = slice(start, start + ROW_CHUNK)
        turns = jnp.dot(turns_ref[rows, :], levels, preferred_element_type=F32)
        features_ref[rows, :] = cosine(turns)
    for start in range(0, exponent_ref.shape[0], ROW_CHUNK):
        rows = slice(start, start + ROW_CHUNK)
        exponent = jnp.dot(exponent_ref[rows, :], levels, preferred_element_type=F32)
        kernel_ref[rows, :] = jnp.exp2(exponent).astype(BF16)


def tiles(turns, exponent, levels, chunk):
    feats, obs = turns.shape[0], exponent.shape[0]
    cands = levels.shape[1] // CHUNKS
    steps = cands // CAND_TILE
    return pl.pallas_call(
        tile_kernel,
        out_shape=(
            jax.ShapeDtypeStruct((feats, cands), BF16),
            jax.ShapeDtypeStruct((obs, cands), BF16),
        ),
        grid=(steps,),
        in_specs=[
            whole(),
            whole(),
            pl.BlockSpec((LANES, CAND_TILE), lambda i: (0, i + chunk * steps)),
        ],
        out_specs=(
            pl.BlockSpec((feats, CAND_TILE), lambda i: (0, i)),
            pl.BlockSpec((obs, CAND_TILE), lambda i: (0, i)),
        ),
        compiler_params=params(),
        cost_estimate=pl.CostEstimate(
            flops=24 * (feats + obs) * cands,
            transcendentals=obs * cands,
            bytes_accessed=2 * (feats + obs) * cands,
        ),
    )(turns, exponent, levels)


def order_kernel(near_ref, far_ref, out_ref):
    rows, half = out_ref.shape[0], near_ref.shape[0] // WIDTHS
    block = rows // WIDTHS
    shard = rows // (WIDTHS * DEPTHS * CORES)
    across, mine = lax.axis_index("rows"), lax.axis_index("cand")
    row = lax.broadcasted_iota(jnp.int32, (block, block), 0)
    column = lax.broadcasted_iota(jnp.int32, (block, block), 1)
    offset = (row // shard) ^ (mine & (DEPTHS * CORES - 1))
    depth = offset // CORES
    depth = jnp.where(depth < DEPTHS // 2, depth, depth ^ (DEPTHS // 2 - 1))
    source = ((offset & (CORES - 1)) * DEPTHS + depth) * shard + (row & (shard - 1))
    chosen = (source == column).astype(F32).astype(BF16)
    for target in range(WIDTHS):
        width = ((across + target) & (WIDTHS - 1)) ^ (mine // (DEPTHS * CORES))
        width = width ^ (width // 2)
        held = pl.ds(pl.multiple_of(width * half, half), half)
        lines = jnp.concatenate([near_ref[held, :], far_ref[held, :]], axis=0)
        out_ref[target * block : (target + 1) * block, :] = jnp.dot(
            chosen, lines, preferred_element_type=F32
        ).astype(BF16)


def in_order(near, far):
    rows, columns = 2 * near.shape[0], near.shape[1]
    return pl.pallas_call(
        order_kernel,
        out_shape=jax.ShapeDtypeStruct((rows, columns), BF16),
        in_specs=[whole(), whole()],
        out_specs=whole(),
        compiler_params=params(),
        cost_estimate=pl.CostEstimate(
            flops=2 * rows * rows * columns, transcendentals=0, bytes_accessed=4 * rows * columns
        ),
    )(near, far)


def prior_kernel(coef_ref, *refs):
    *features, out_ref = refs
    cands = features[0].shape[1]
    for chunk, feature_ref in enumerate(features):
        out_ref[:, chunk * cands : (chunk + 1) * cands] = jnp.dot(
            coef_ref[...], feature_ref[...], preferred_element_type=F32
        )


def cross_kernel(weight_ref, prior_ref, *refs):
    kernels, outs = refs[:-WIDTHS], refs[-WIDTHS:]
    block = weight_ref.shape[0] // WIDTHS
    cands = kernels[0].shape[1]
    for chunk, kernel_ref in enumerate(kernels):
        cols = slice(chunk * cands, (chunk + 1) * cands)
        total = prior_ref[:, cols] + jnp.dot(
            weight_ref[...], kernel_ref[...], preferred_element_type=F32
        )
        for target, out in enumerate(outs):
            rows = slice(target * block, (target + 1) * block)
            out[:, cols] = total[rows].astype(out.dtype)


def prior_product(coefs, features):
    rows, cands = coefs.shape[0], len(features) * features[0].shape[1]
    feats = coefs.shape[1]
    return pl.pallas_call(
        prior_kernel,
        out_shape=jax.ShapeDtypeStruct((rows, cands), F32),
        in_specs=[whole()] * (1 + len(features)),
        out_specs=whole(),
        compiler_params=params(),
        cost_estimate=pl.CostEstimate(
            flops=2 * rows * feats * cands, transcendentals=0, bytes_accessed=2 * feats * cands
        ),
    )(coefs, *features)


def cross_product(weights, prior, kernels):
    rows, cands = prior.shape
    obs = weights.shape[1]
    shape = (rows // WIDTHS, cands)
    out_shapes = (jax.ShapeDtypeStruct(shape, F32),) + (jax.ShapeDtypeStruct(shape, BF16),) * (
        WIDTHS - 1
    )
    return pl.pallas_call(
        cross_kernel,
        out_shape=out_shapes,
        in_specs=[whole()] * (2 + len(kernels)),
        out_specs=(whole(),) * WIDTHS,
        compiler_params=params(),
        cost_estimate=pl.CostEstimate(
            flops=2 * rows * obs * cands, transcendentals=0, bytes_accessed=8 * rows * cands
        ),
    )(weights, prior, *kernels)


def total_kernel(first, *refs):
    *parts, out_ref, sums, sem = refs
    total = parts[0][...]
    for part in parts[1:WIDTHS]:
        total = total + part[...].astype(F32)
    sums[...] = total
    copy = pltpu.make_async_copy(sums, out_ref.at[:, first : first + total.shape[1]], sem)
    copy.start()
    copy.wait()


def total(parts, first, cands, held):
    rows, columns = parts[0].shape
    extra = [] if held is None else [held]
    return pl.pallas_call(
        functools.partial(total_kernel, first),
        out_shape=jax.ShapeDtypeStruct((rows, cands), F32),
        in_specs=[whole()] * len(parts) + [pl.BlockSpec(memory_space=pl.ANY)] * len(extra),
        out_specs=pl.BlockSpec(memory_space=pl.ANY),
        scratch_shapes=[pltpu.VMEM((rows, columns), F32), pltpu.SemaphoreType.DMA(())],
        input_output_aliases={len(parts): 0} if extra else {},
        compiler_params=params(),
        cost_estimate=pl.CostEstimate(
            flops=3 * rows * columns, transcendentals=0, bytes_accessed=14 * rows * columns
        ),
    )(*parts, *extra)


def exchange_pairs(mask):
    devices = WIDTHS * DEPTHS * CORES
    return [(i, i ^ mask) for i in range(devices)]


def stack_kernel(*refs):
    *pieces, out_ref, rows = refs
    count = pieces[0].shape[0]
    if count % 16 == 0:
        for index, piece in enumerate(pieces):
            out_ref[index * count : (index + 1) * count, :] = piece[...]
        return
    for index, piece in enumerate(pieces):
        rows[index * count : (index + 1) * count, :] = piece[...].astype(F32)
    out_ref[...] = rows[...].astype(BF16)


def stack(pieces):
    shape = (len(pieces) * pieces[0].shape[0], pieces[0].shape[1])
    return pl.pallas_call(
        stack_kernel,
        out_shape=jax.ShapeDtypeStruct(shape, BF16),
        in_specs=[whole()] * len(pieces),
        out_specs=whole(),
        scratch_shapes=[pltpu.VMEM(shape, F32)],
        compiler_params=params(),
        cost_estimate=pl.CostEstimate(
            flops=0, transcendentals=0, bytes_accessed=4 * shape[0] * shape[1]
        ),
    )(*pieces)


def spread(piece, at_once):
    def swap(held, pairs):
        return lax.ppermute(held, "cand", pairs)

    held = piece
    for hop in (1, 2, 7):
        other = swap(held, exchange_pairs(hop * CORES))
        held = stack([held, other])
    step = DEPTHS * CORES
    if at_once:
        others = [swap(held, exchange_pairs(hop * step)) for hop in (1, 3, 2)]
        near = stack([held] + others)
    else:
        near = stack([held, swap(held, exchange_pairs(step))])
        near = stack([near, swap(near, exchange_pairs(3 * step))])
    return near, swap(near, exchange_pairs(1))


def exact_lines(left, lines):
    rows = left.shape[0]
    lines[...] = jnp.zeros_like(lines)
    for index, piece in enumerate(three_pieces(left)):
        lines[index * rows : (index + 1) * rows, :] = piece
    return lines[...].astype(BF16)


def exact_dot(lines, rows, right):
    total = None
    for piece, count in zip(three_pieces(right)[::-1], (1, 2, 3)):
        product = jnp.dot(lines, piece.astype(BF16), preferred_element_type=F32)
        for index in reversed(range(count)):
            term = product[index * rows : (index + 1) * rows]
            total = term if total is None else total + term
    return total


def solve_kernel(
    section, whitened_ref, inverse_ref, factor_ref, carried_ref, weights_ref, *rest
):
    *update_ref, solved_ref, lines = rest
    count, width = whitened_ref.shape
    active = lax.axis_index("rows") == section

    @pl.when(active)
    def _():
        remaining = whitened_ref[...]
        if carried_ref is not None:
            remaining = remaining - carried_ref[:, section * width : (section + 1) * width]
        solved = exact_dot(exact_lines(remaining, lines), count, inverse_ref[...])
        solved_ref[...] = solved.astype(BF16)
        if section > 0:
            left = exact_lines(solved, lines)

            @pl.loop(0, section)
            def _(earlier):
                cols = pl.ds(pl.multiple_of(earlier * width, width), width)
                update = exact_dot(left, count, factor_ref[:, cols])
                if carried_ref is not None:
                    update = update + carried_ref[:, cols]
                update_ref[0][:, cols] = update

    if weights_ref is not None:
        @pl.when(jnp.logical_not(active))
        def _():
            solved_ref[...] = weights_ref[...]


def solve(section, whitened, carried, weights, diag_inv, factor_rows):
    count, width = whitened.shape
    out_shape = [jax.ShapeDtypeStruct((count, width), BF16)]
    if section > 0:
        out_shape.insert(0, jax.ShapeDtypeStruct((count, section * width), F32))
    first = carried is None

    def kernel(whitened_ref, inverse_ref, factor_ref, *refs):
        if first:
            refs = (None, None) + refs
        solve_kernel(section, whitened_ref, inverse_ref, factor_ref, *refs)

    held = [] if first else [carried, weights]
    columns = (section + 1) * width
    results = pl.pallas_call(
        kernel,
        out_shape=out_shape,
        in_specs=[whole()] * (3 + len(held)),
        out_specs=[whole()] * len(out_shape),
        scratch_shapes=[pltpu.VMEM((16, width), F32)],
        compiler_params=params(),
        cost_estimate=pl.CostEstimate(
            flops=2 * 36 * width * columns, transcendentals=0, bytes_accessed=4 * width * columns
        ),
    )(whitened, diag_inv, factor_rows, *held)
    return results if section > 0 else (None, results[0])


def solve_chain(whitened, factor_rows, diag_inv):
    sections = lax.axis_size("rows")
    carried = weights = None
    for section in reversed(range(sections)):
        carried, weights = solve(section, whitened, carried, weights, diag_inv, factor_rows)
        if section > 0:
            carried = lax.ppermute(carried, "rows", [(section, section - 1)])
    return weights


def body(
    whitened,
    factor_rows,
    diag_inv,
    observed,
    inv_length,
    grid_coords,
    frequencies,
    phases,
    prior_coef,
):
    turns, exponent, levels, inverse, factor = prepare(
        frequencies, phases, observed, inv_length, grid_coords, diag_inv, factor_rows
    )
    coef_near, coef_far = spread(prior_coef, False)
    weights = solve_chain(whitened, factor, inverse)
    weight_near, weight_far = spread(weights, True)
    made = [tiles(turns, exponent, levels, chunk) for chunk in range(CHUNKS)]
    coefs = in_order(coef_near, coef_far)
    solved = in_order(weight_near, weight_far)
    rows = lax.axis_size("rows")
    result = None
    for first, last in PARTS:
        mine = made[first:last]
        prior = prior_product(coefs, [m[0] for m in mine])
        own, *away = cross_product(solved, prior, [m[1] for m in mine])
        arrived = []
        for shift, block in enumerate(away, 1):
            pairs = [(i, (i + shift) % rows) for i in range(rows)]
            arrived.append(lax.ppermute(block, "rows", pairs))
        cands = grid_coords.shape[1]
        start = first * (cands // CHUNKS)
        result = total([own] + arrived, start, cands, result)
    return result.T


def solution(mesh):
    in_specs = (
        P("cand", "rows"),
        P("rows", None),
        P("rows", None),
        P(None, "rows"),
        P(),
        P(None, "cand"),
        P(None, "rows"),
        P("rows"),
        P("cand", "rows"),
    )
    out_specs = P("cand", "rows")

    return jax.shard_map(body, mesh=mesh, in_specs=in_specs, out_specs=out_specs, check_vma=False)
```

```python
import functools

import jax
import jax.numpy as jnp
from jax import lax
from jax.experimental import pallas as pl
from jax.experimental.pallas import tpu as pltpu
from jax.sharding import PartitionSpec as P

F32 = jnp.float32
BF16 = jnp.bfloat16
GRID = 21
DIM = 22
CORES = 2
DEPTHS = 8
WIDTHS = 4
LANES = 128
STRIPE = 24
ROW_CHUNK = 256
CAND_TILE = 256
CHUNKS = 8
PARTS = ((0, 6), (6, 8))
VMEM_BYTES = 16 * 2**20
LOG2E = 1.4426950408889634
INV_TURN = 0.15915494309189535
SINE = (0.55535848, -0.91343016, 0.4493464, -0.09804192)


def params(limit=VMEM_BYTES):
    return pltpu.CompilerParams(vmem_limit_bytes=limit)


def whole():
    return pl.BlockSpec(memory_space=pltpu.VMEM)


def three_pieces(values):
    high = values.astype(BF16).astype(F32)
    rest = values - high
    middle = rest.astype(BF16).astype(F32)
    return high, middle, (rest - middle).astype(BF16).astype(F32)


def stack_pieces(scratch, values, tail):
    scratch[...] = jnp.zeros_like(scratch)
    for piece, part in enumerate(values):
        scratch[piece * STRIPE : piece * STRIPE + DIM, :] = part
    row = lax.broadcasted_iota(jnp.int32, (8, scratch.shape[1]), 0)
    block = jnp.zeros((8, scratch.shape[1]), F32)
    for index, line in enumerate(tail):
        block = jnp.where(row == index, line, block)
    scratch[3 * STRIPE : 3 * STRIPE + 8, :] = block


def prepare_kernel(*refs):
    sources, refs = refs[:7], refs[7:]
    (turns_ref, exponent_ref, levels_ref, inverse_ref, factor_ref), refs = refs[:5], refs[5:]
    (freq_ref, phase_ref, observed_ref, scale_ref, grid_ref), refs = refs[:5], refs[5:]
    wide, narrow, tall, sems = refs
    targets = (freq_ref, phase_ref, observed_ref, scale_ref, grid_ref, inverse_ref, factor_ref)
    copies = [
        pltpu.make_async_copy(
            source.at[:, : target.shape[1]], target, sems.at[index]
        )
        for index, (source, target) in enumerate(zip(sources, targets))
    ]
    for copy in copies:
        copy.start()
    for copy in copies[:5]:
        copy.wait()
    stack_pieces(
        wide,
        three_pieces(freq_ref[...] * (INV_TURN / (GRID - 1))),
        three_pieces(phase_ref[...] * INV_TURN),
    )
    for start in range(0, wide.shape[1], 512):
        turns_ref[start : start + 512, :] = wide[:, start : start + 512].T.astype(BF16)
    scale = jnp.broadcast_to(scale_ref[...], (DIM, DIM))
    line = lax.broadcasted_iota(jnp.int32, (DIM, DIM), 0)
    lane = lax.broadcasted_iota(jnp.int32, (DIM, DIM), 1)
    scale = jnp.sum(jnp.where(line == lane, scale, 0.0), axis=1, keepdims=True)
    squares = scale * scale
    observed = observed_ref[...]
    ones = jnp.ones((1, narrow.shape[1]), F32)
    norm = jnp.sum(observed * observed * squares, axis=0, keepdims=True) * (-0.5 * LOG2E)
    stack_pieces(
        narrow,
        three_pieces(observed * squares * (LOG2E / (GRID - 1))),
        three_pieces(norm) + (ones, ones, ones),
    )
    exponent_ref[...] = narrow[...].T.astype(BF16)
    levels = grid_ref[...].astype(F32)
    ones = jnp.ones((1, tall.shape[1]), F32)
    norm = jnp.sum(levels * levels * squares, axis=0, keepdims=True) * (
        -0.5 * LOG2E / (GRID - 1) ** 2
    )
    stack_pieces(tall, (levels, levels, levels), (ones, ones, ones) + three_pieces(norm))
    levels_ref[...] = tall[...].astype(BF16)
    for copy in copies[5:]:
        copy.wait()


def prepare(frequencies, phases, observed, inv_length, grid_coords, diag_inv, factor_rows):
    feats, obs, cands = frequencies.shape[1], observed.shape[1], grid_coords.shape[1]
    arrays = (frequencies, phases[None, :], observed, inv_length[None, :], grid_coords)
    earlier = factor_rows.shape[1] - diag_inv.shape[1]
    return pl.pallas_call(
        prepare_kernel,
        out_shape=(
            jax.ShapeDtypeStruct((feats, LANES), BF16),
            jax.ShapeDtypeStruct((obs, LANES), BF16),
            jax.ShapeDtypeStruct((LANES, cands), BF16),
            jax.ShapeDtypeStruct(diag_inv.shape, F32),
            jax.ShapeDtypeStruct((factor_rows.shape[0], earlier), F32),
        ),
        in_specs=[pl.BlockSpec(memory_space=pl.ANY)] * 7,
        out_specs=(whole(),) * 5,
        scratch_shapes=[pltpu.VMEM(array.shape, array.dtype) for array in arrays]
        + [
            pltpu.VMEM((LANES, feats), F32),
            pltpu.VMEM((LANES, obs), F32),
            pltpu.VMEM((LANES, cands), F32),
            pltpu.SemaphoreType.DMA((7,)),
        ],
        compiler_params=params(),
        cost_estimate=pl.CostEstimate(flops=10**7, transcendentals=0, bytes_accessed=8 * 2**20),
        name="prepare",
    )(
        *(
            pltpu.with_memory_space_constraint(array, pltpu.HBM)
            for array in (*arrays, diag_inv, factor_rows)
        )
    )


def cosine(turns):
    near = turns - jnp.round(turns)
    square = near * near
    poly = ((SINE[3] * square + SINE[2]) * square + SINE[1]) * square + SINE[0]
    sine = near * poly
    return (0.015625 - sine * sine).astype(BF16)


def tile_kernel(turns_ref, exponent_ref, levels_ref, features_ref, kernel_ref):
    levels = levels_ref[...]
    for start in range(0, turns_ref.shape[0], ROW_CHUNK):
        rows = slice(start, start + ROW_CHUNK)
        turns = jnp.dot(turns_ref[rows, :], levels, preferred_element_type=F32)
        features_ref[rows, :] = cosine(turns)
    for start in range(0, exponent_ref.shape[0], ROW_CHUNK):
        rows = slice(start, start + ROW_CHUNK)
        exponent = jnp.dot(exponent_ref[rows, :], levels, preferred_element_type=F32)
        kernel_ref[rows, :] = jnp.exp2(exponent).astype(BF16)


def tiles(turns, exponent, levels, chunk):
    feats, obs = turns.shape[0], exponent.shape[0]
    cands = levels.shape[1] // CHUNKS
    steps = cands // CAND_TILE
    return pl.pallas_call(
        tile_kernel,
        out_shape=(
            jax.ShapeDtypeStruct((feats, cands), BF16),
            jax.ShapeDtypeStruct((obs, cands), BF16),
        ),
        grid=(steps,),
        in_specs=[
            whole(),
            whole(),
            pl.BlockSpec((LANES, CAND_TILE), lambda i: (0, i + chunk * steps)),
        ],
        out_specs=(
            pl.BlockSpec((feats, CAND_TILE), lambda i: (0, i)),
            pl.BlockSpec((obs, CAND_TILE), lambda i: (0, i)),
        ),
        compiler_params=params(),
        cost_estimate=pl.CostEstimate(
            flops=24 * (feats + obs) * cands,
            transcendentals=obs * cands,
            bytes_accessed=2 * (feats + obs) * cands,
        ),
    )(turns, exponent, levels)


def order_kernel(near_ref, far_ref, out_ref):
    rows, half = out_ref.shape[0], near_ref.shape[0] // WIDTHS
    block = rows // WIDTHS
    shard = rows // (WIDTHS * DEPTHS * CORES)
    across, mine = lax.axis_index("rows"), lax.axis_index("cand")
    row = lax.broadcasted_iota(jnp.int32, (block, block), 0)
    column = lax.broadcasted_iota(jnp.int32, (block, block), 1)
    offset = (row // shard) ^ (mine & (DEPTHS * CORES - 1))
    depth = offset // CORES
    depth = jnp.where(depth < DEPTHS // 2, depth, depth ^ (DEPTHS // 2 - 1))
    source = ((offset & (CORES - 1)) * DEPTHS + depth) * shard + (row & (shard - 1))
    chosen = (source == column).astype(F32).astype(BF16)
    for target in range(WIDTHS):
        width = ((across + target) & (WIDTHS - 1)) ^ (mine // (DEPTHS * CORES))
        width = width ^ (width // 2)
        held = pl.ds(pl.multiple_of(width * half, half), half)
        lines = jnp.concatenate([near_ref[held, :], far_ref[held, :]], axis=0)
        out_ref[target * block : (target + 1) * block, :] = jnp.dot(
            chosen, lines, preferred_element_type=F32
        ).astype(BF16)


def in_order(near, far):
    rows, columns = 2 * near.shape[0], near.shape[1]
    return pl.pallas_call(
        order_kernel,
        out_shape=jax.ShapeDtypeStruct((rows, columns), BF16),
        in_specs=[whole(), whole()],
        out_specs=whole(),
        compiler_params=params(),
        cost_estimate=pl.CostEstimate(
            flops=2 * rows * rows * columns, transcendentals=0, bytes_accessed=4 * rows * columns
        ),
    )(near, far)


def prior_kernel(coef_ref, *refs):
    *features, out_ref = refs
    cands = features[0].shape[1]
    for chunk, feature_ref in enumerate(features):
        out_ref[:, chunk * cands : (chunk + 1) * cands] = jnp.dot(
            coef_ref[...], feature_ref[...], preferred_element_type=F32
        )


def cross_kernel(weight_ref, prior_ref, *refs):
    kernels, (own_ref, up_ref, down_ref, far_up_ref, far_down_ref) = refs[:-5], refs[-5:]
    block = weight_ref.shape[0] // WIDTHS
    cands = kernels[0].shape[1]
    half = far_up_ref.shape[1]
    for chunk, kernel_ref in enumerate(kernels):
        cols = slice(chunk * cands, (chunk + 1) * cands)
        total = prior_ref[:, cols] + jnp.dot(
            weight_ref[...], kernel_ref[...], preferred_element_type=F32
        )
        own_ref[:, cols] = total[:block]
        up_ref[:, cols] = total[block : 2 * block]
        down_ref[:, cols] = total[3 * block :]
        far_ref, first = (far_up_ref, 0) if cols.start < half else (far_down_ref, half)
        far_ref[:, cols.start - first : cols.stop - first] = total[2 * block : 3 * block].astype(BF16)


def merge_kernel(up_ref, down_ref, far_up_ref, far_down_ref, up_out, down_out):
    half = far_up_ref.shape[1]
    up_out[:, :half] = (up_ref[:, :half] + far_up_ref[...].astype(F32)).astype(BF16)
    up_out[:, half:] = up_ref[:, half:].astype(BF16)
    down_out[:, :half] = down_ref[:, :half].astype(BF16)
    down_out[:, half:] = (down_ref[:, half:] + far_down_ref[...].astype(F32)).astype(BF16)


def merge(up, down, far_up, far_down):
    return pl.pallas_call(
        merge_kernel,
        out_shape=(jax.ShapeDtypeStruct(up.shape, BF16),) * 2,
        in_specs=[whole()] * 4,
        out_specs=(whole(),) * 2,
        compiler_params=params(),
        cost_estimate=pl.CostEstimate(
            flops=2 * up.size, transcendentals=0, bytes_accessed=14 * up.size
        ),
    )(up, down, far_up, far_down)


def prior_product(coefs, features):
    rows, cands = coefs.shape[0], len(features) * features[0].shape[1]
    feats = coefs.shape[1]
    return pl.pallas_call(
        prior_kernel,
        out_shape=jax.ShapeDtypeStruct((rows, cands), F32),
        in_specs=[whole()] * (1 + len(features)),
        out_specs=whole(),
        compiler_params=params(),
        cost_estimate=pl.CostEstimate(
            flops=2 * rows * feats * cands, transcendentals=0, bytes_accessed=2 * feats * cands
        ),
    )(coefs, *features)


def cross_product(weights, prior, kernels):
    rows, cands = prior.shape
    obs = weights.shape[1]
    block = rows // WIDTHS
    out_shapes = (jax.ShapeDtypeStruct((block, cands), F32),) * 3 + (
        jax.ShapeDtypeStruct((block, cands // 2), BF16),
    ) * 2
    return pl.pallas_call(
        cross_kernel,
        out_shape=out_shapes,
        in_specs=[whole()] * (2 + len(kernels)),
        out_specs=(whole(),) * 5,
        compiler_params=params(),
        cost_estimate=pl.CostEstimate(
            flops=2 * rows * obs * cands, transcendentals=0, bytes_accessed=8 * rows * cands
        ),
    )(weights, prior, *kernels)


def total_kernel(first, *refs):
    *parts, out_ref, sums, sem = refs
    total = parts[0][...]
    for part in parts[1:3]:
        total = total + part[...].astype(F32)
    sums[...] = total
    copy = pltpu.make_async_copy(sums, out_ref.at[:, first : first + total.shape[1]], sem)
    copy.start()
    copy.wait()


def total(parts, first, cands, held):
    rows, columns = parts[0].shape
    extra = [] if held is None else [held]
    return pl.pallas_call(
        functools.partial(total_kernel, first),
        out_shape=jax.ShapeDtypeStruct((rows, cands), F32),
        in_specs=[whole()] * len(parts) + [pl.BlockSpec(memory_space=pl.ANY)] * len(extra),
        out_specs=pl.BlockSpec(memory_space=pl.ANY),
        scratch_shapes=[pltpu.VMEM((rows, columns), F32), pltpu.SemaphoreType.DMA(())],
        input_output_aliases={len(parts): 0} if extra else {},
        compiler_params=params(),
        cost_estimate=pl.CostEstimate(
            flops=3 * rows * columns, transcendentals=0, bytes_accessed=14 * rows * columns
        ),
    )(*parts, *extra)


def exchange_pairs(mask):
    devices = WIDTHS * DEPTHS * CORES
    return [(i, i ^ mask) for i in range(devices)]


def stack_kernel(*refs):
    *pieces, out_ref, rows = refs
    count = pieces[0].shape[0]
    if count % 16 == 0:
        for index, piece in enumerate(pieces):
            out_ref[index * count : (index + 1) * count, :] = piece[...]
        return
    for index, piece in enumerate(pieces):
        rows[index * count : (index + 1) * count, :] = piece[...].astype(F32)
    out_ref[...] = rows[...].astype(BF16)


def stack(pieces):
    shape = (len(pieces) * pieces[0].shape[0], pieces[0].shape[1])
    return pl.pallas_call(
        stack_kernel,
        out_shape=jax.ShapeDtypeStruct(shape, BF16),
        in_specs=[whole()] * len(pieces),
        out_specs=whole(),
        scratch_shapes=[pltpu.VMEM(shape, F32)],
        compiler_params=params(),
        cost_estimate=pl.CostEstimate(
            flops=0, transcendentals=0, bytes_accessed=4 * shape[0] * shape[1]
        ),
    )(*pieces)


def spread(piece):
    def swap(held, pairs):
        return lax.ppermute(held, "cand", pairs)

    held = piece
    for hop in (1, 2, 7):
        other = swap(held, exchange_pairs(hop * CORES))
        held = stack([held, other])
    step = DEPTHS * CORES
    near = stack([held, swap(held, exchange_pairs(step))])
    near = stack([near, swap(near, exchange_pairs(3 * step))])
    return near, swap(near, exchange_pairs(1))


def exact_lines(left, lines):
    rows = left.shape[0]
    lines[...] = jnp.zeros_like(lines)
    for index, piece in enumerate(three_pieces(left)):
        lines[index * rows : (index + 1) * rows, :] = piece
    return lines[...].astype(BF16)


def exact_dot(lines, rows, right):
    total = None
    for piece, count in zip(three_pieces(right)[::-1], (1, 2, 3)):
        product = jnp.dot(lines, piece.astype(BF16), preferred_element_type=F32)
        for index in reversed(range(count)):
            term = product[index * rows : (index + 1) * rows]
            total = term if total is None else total + term
    return total


def solve_kernel(
    section, whitened_ref, inverse_ref, factor_ref, carried_ref, weights_ref, *rest
):
    *update_ref, solved_ref, lines = rest
    count, width = whitened_ref.shape
    active = lax.axis_index("rows") == section

    @pl.when(active)
    def _():
        remaining = whitened_ref[...]
        if carried_ref is not None:
            remaining = remaining - carried_ref[:, section * width : (section + 1) * width]
        solved = exact_dot(exact_lines(remaining, lines), count, inverse_ref[...])
        solved_ref[...] = solved.astype(BF16)
        if section > 0:
            left = exact_lines(solved, lines)

            @pl.loop(0, section)
            def _(earlier):
                cols = pl.ds(pl.multiple_of(earlier * width, width), width)
                update = exact_dot(left, count, factor_ref[:, cols])
                if carried_ref is not None:
                    update = update + carried_ref[:, cols]
                update_ref[0][:, cols] = update

    if weights_ref is not None:
        @pl.when(jnp.logical_not(active))
        def _():
            solved_ref[...] = weights_ref[...]


def solve(section, whitened, carried, weights, diag_inv, factor_rows):
    count, width = whitened.shape
    out_shape = [jax.ShapeDtypeStruct((count, width), BF16)]
    if section > 0:
        out_shape.insert(0, jax.ShapeDtypeStruct((count, section * width), F32))
    first = carried is None

    def kernel(whitened_ref, inverse_ref, factor_ref, *refs):
        if first:
            refs = (None, None) + refs
        solve_kernel(section, whitened_ref, inverse_ref, factor_ref, *refs)

    held = [] if first else [carried, weights]
    columns = (section + 1) * width
    results = pl.pallas_call(
        kernel,
        out_shape=out_shape,
        in_specs=[whole()] * (3 + len(held)),
        out_specs=[whole()] * len(out_shape),
        scratch_shapes=[pltpu.VMEM((16, width), F32)],
        compiler_params=params(),
        cost_estimate=pl.CostEstimate(
            flops=2 * 36 * width * columns, transcendentals=0, bytes_accessed=4 * width * columns
        ),
    )(whitened, diag_inv, factor_rows, *held)
    return results if section > 0 else (None, results[0])


def solve_chain(whitened, factor_rows, diag_inv):
    sections = lax.axis_size("rows")
    carried = weights = None
    for section in reversed(range(sections)):
        carried, weights = solve(section, whitened, carried, weights, diag_inv, factor_rows)
        if section > 0:
            carried = lax.ppermute(carried, "rows", [(section, section - 1)])
    return weights


def body(
    whitened,
    factor_rows,
    diag_inv,
    observed,
    inv_length,
    grid_coords,
    frequencies,
    phases,
    prior_coef,
):
    turns, exponent, levels, inverse, factor = prepare(
        frequencies, phases, observed, inv_length, grid_coords, diag_inv, factor_rows
    )
    coef_near, coef_far = spread(prior_coef)
    weights = solve_chain(whitened, factor, inverse)
    weight_near, weight_far = spread(weights)
    made = [tiles(turns, exponent, levels, chunk) for chunk in range(CHUNKS)]
    coefs = in_order(coef_near, coef_far)
    solved = in_order(weight_near, weight_far)
    rows = lax.axis_size("rows")

    def beside(block, step):
        return lax.ppermute(block, "rows", [(i, (i + step) % rows) for i in range(rows)])

    result = None
    for first, last in PARTS:
        mine = made[first:last]
        prior = prior_product(coefs, [m[0] for m in mine])
        kernels = [m[1] for m in mine]
        own, up, down, far_up, far_down = cross_product(solved, prior, kernels)
        far_up = beside(far_up, 1)
        far_down = beside(far_down, -1)
        up, down = merge(up, down, far_up, far_down)
        arrived = [beside(up, 1), beside(down, -1)]
        cands = grid_coords.shape[1]
        start = first * (cands // CHUNKS)
        result = total([own] + arrived, start, cands, result)
    return result.T


def solution(mesh):
    in_specs = (
        P("cand", "rows"),
        P("rows", None),
        P("rows", None),
        P(None, "rows"),
        P(),
        P(None, "cand"),
        P(None, "rows"),
        P("rows"),
        P("cand", "rows"),
    )
    out_specs = P("cand", "rows")

    return jax.shard_map(body, mesh=mesh, in_specs=in_specs, out_specs=out_specs, check_vma=False)
```

```python
import functools

import jax
import jax.numpy as jnp
from jax import lax
from jax.experimental import pallas as pl
from jax.experimental.pallas import tpu as pltpu
from jax.sharding import PartitionSpec as P

F32 = jnp.float32
BF16 = jnp.bfloat16
GRID = 21
DIM = 22
CORES = 2
DEPTHS = 8
WIDTHS = 4
LANES = 128
STRIPE = 24
ROW_CHUNK = 256
CAND_TILE = 256
CHUNKS = 8
PARTS = ((0, 5), (5, 8))
VMEM_BYTES = 16 * 2**20
LOG2E = 1.4426950408889634
INV_TURN = 0.15915494309189535
SINE = (0.55535848, -0.91343016, 0.4493464, -0.09804192)


def params(limit=VMEM_BYTES):
    return pltpu.CompilerParams(vmem_limit_bytes=limit)


def whole():
    return pl.BlockSpec(memory_space=pltpu.VMEM)


def three_pieces(values):
    high = values.astype(BF16).astype(F32)
    rest = values - high
    middle = rest.astype(BF16).astype(F32)
    return high, middle, (rest - middle).astype(BF16).astype(F32)


def stack_pieces(scratch, values, tail):
    scratch[...] = jnp.zeros_like(scratch)
    for piece, part in enumerate(values):
        scratch[piece * STRIPE : piece * STRIPE + DIM, :] = part
    row = lax.broadcasted_iota(jnp.int32, (8, scratch.shape[1]), 0)
    block = jnp.zeros((8, scratch.shape[1]), F32)
    for index, line in enumerate(tail):
        block = jnp.where(row == index, line, block)
    scratch[3 * STRIPE : 3 * STRIPE + 8, :] = block


def prepare_kernel(*refs):
    sources, refs = refs[:7], refs[7:]
    (turns_ref, exponent_ref, levels_ref, inverse_ref, factor_ref), refs = refs[:5], refs[5:]
    (freq_ref, phase_ref, observed_ref, scale_ref, grid_ref), refs = refs[:5], refs[5:]
    wide, narrow, tall, sems = refs
    targets = (freq_ref, phase_ref, observed_ref, scale_ref, grid_ref, inverse_ref, factor_ref)
    copies = [
        pltpu.make_async_copy(
            source.at[:, : target.shape[1]], target, sems.at[index]
        )
        for index, (source, target) in enumerate(zip(sources, targets))
    ]
    for copy in copies:
        copy.start()
    for copy in copies[:5]:
        copy.wait()
    stack_pieces(
        wide,
        three_pieces(freq_ref[...] * (INV_TURN / (GRID - 1))),
        three_pieces(phase_ref[...] * INV_TURN),
    )
    for start in range(0, wide.shape[1], 512):
        turns_ref[start : start + 512, :] = wide[:, start : start + 512].T.astype(BF16)
    scale = jnp.broadcast_to(scale_ref[...], (DIM, DIM))
    line = lax.broadcasted_iota(jnp.int32, (DIM, DIM), 0)
    lane = lax.broadcasted_iota(jnp.int32, (DIM, DIM), 1)
    scale = jnp.sum(jnp.where(line == lane, scale, 0.0), axis=1, keepdims=True)
    squares = scale * scale
    observed = observed_ref[...]
    ones = jnp.ones((1, narrow.shape[1]), F32)
    norm = jnp.sum(observed * observed * squares, axis=0, keepdims=True) * (-0.5 * LOG2E)
    stack_pieces(
        narrow,
        three_pieces(observed * squares * (LOG2E / (GRID - 1))),
        three_pieces(norm) + (ones, ones, ones),
    )
    exponent_ref[...] = narrow[...].T.astype(BF16)
    levels = grid_ref[...].astype(F32)
    ones = jnp.ones((1, tall.shape[1]), F32)
    norm = jnp.sum(levels * levels * squares, axis=0, keepdims=True) * (
        -0.5 * LOG2E / (GRID - 1) ** 2
    )
    stack_pieces(tall, (levels, levels, levels), (ones, ones, ones) + three_pieces(norm))
    levels_ref[...] = tall[...].astype(BF16)
    for copy in copies[5:]:
        copy.wait()


def prepare(frequencies, phases, observed, inv_length, grid_coords, diag_inv, factor_rows):
    feats, obs, cands = frequencies.shape[1], observed.shape[1], grid_coords.shape[1]
    arrays = (frequencies, phases[None, :], observed, inv_length[None, :], grid_coords)
    earlier = factor_rows.shape[1] - diag_inv.shape[1]
    return pl.pallas_call(
        prepare_kernel,
        out_shape=(
            jax.ShapeDtypeStruct((feats, LANES), BF16),
            jax.ShapeDtypeStruct((obs, LANES), BF16),
            jax.ShapeDtypeStruct((LANES, cands), BF16),
            jax.ShapeDtypeStruct(diag_inv.shape, F32),
            jax.ShapeDtypeStruct((factor_rows.shape[0], earlier), F32),
        ),
        in_specs=[pl.BlockSpec(memory_space=pl.ANY)] * 7,
        out_specs=(whole(),) * 5,
        scratch_shapes=[pltpu.VMEM(array.shape, array.dtype) for array in arrays]
        + [
            pltpu.VMEM((LANES, feats), F32),
            pltpu.VMEM((LANES, obs), F32),
            pltpu.VMEM((LANES, cands), F32),
            pltpu.SemaphoreType.DMA((7,)),
        ],
        compiler_params=params(),
        cost_estimate=pl.CostEstimate(flops=10**7, transcendentals=0, bytes_accessed=8 * 2**20),
        name="prepare",
    )(
        *(
            pltpu.with_memory_space_constraint(array, pltpu.HBM)
            for array in (*arrays, diag_inv, factor_rows)
        )
    )


def cosine(turns):
    near = turns - jnp.round(turns)
    square = near * near
    poly = ((SINE[3] * square + SINE[2]) * square + SINE[1]) * square + SINE[0]
    sine = near * poly
    return (0.015625 - sine * sine).astype(BF16)


def tile_kernel(turns_ref, exponent_ref, levels_ref, features_ref, kernel_ref):
    levels = levels_ref[...]
    for start in range(0, turns_ref.shape[0], ROW_CHUNK):
        rows = slice(start, start + ROW_CHUNK)
        turns = jnp.dot(turns_ref[rows, :], levels, preferred_element_type=F32)
        features_ref[rows, :] = cosine(turns)
    for start in range(0, exponent_ref.shape[0], ROW_CHUNK):
        rows = slice(start, start + ROW_CHUNK)
        exponent = jnp.dot(exponent_ref[rows, :], levels, preferred_element_type=F32)
        kernel_ref[rows, :] = jnp.exp2(exponent).astype(BF16)


def tiles(turns, exponent, levels, chunk):
    feats, obs = turns.shape[0], exponent.shape[0]
    cands = levels.shape[1] // CHUNKS
    steps = cands // CAND_TILE
    return pl.pallas_call(
        tile_kernel,
        out_shape=(
            jax.ShapeDtypeStruct((feats, cands), BF16),
            jax.ShapeDtypeStruct((obs, cands), BF16),
        ),
        grid=(steps,),
        in_specs=[
            whole(),
            whole(),
            pl.BlockSpec((LANES, CAND_TILE), lambda i: (0, i + chunk * steps)),
        ],
        out_specs=(
            pl.BlockSpec((feats, CAND_TILE), lambda i: (0, i)),
            pl.BlockSpec((obs, CAND_TILE), lambda i: (0, i)),
        ),
        compiler_params=params(),
        cost_estimate=pl.CostEstimate(
            flops=24 * (feats + obs) * cands,
            transcendentals=obs * cands,
            bytes_accessed=2 * (feats + obs) * cands,
        ),
    )(turns, exponent, levels)


def order_kernel(near_ref, far_ref, out_ref):
    rows, half = out_ref.shape[0], near_ref.shape[0] // WIDTHS
    block = rows // WIDTHS
    shard = rows // (WIDTHS * DEPTHS * CORES)
    across, mine = lax.axis_index("rows"), lax.axis_index("cand")
    row = lax.broadcasted_iota(jnp.int32, (block, block), 0)
    column = lax.broadcasted_iota(jnp.int32, (block, block), 1)
    offset = (row // shard) ^ (mine & (DEPTHS * CORES - 1))
    depth = offset // CORES
    depth = jnp.where(depth < DEPTHS // 2, depth, depth ^ (DEPTHS // 2 - 1))
    source = ((offset & (CORES - 1)) * DEPTHS + depth) * shard + (row & (shard - 1))
    chosen = (source == column).astype(F32).astype(BF16)
    for target in range(WIDTHS):
        width = ((across + target) & (WIDTHS - 1)) ^ (mine // (DEPTHS * CORES))
        width = width ^ (width // 2)
        held = pl.ds(pl.multiple_of(width * half, half), half)
        lines = jnp.concatenate([near_ref[held, :], far_ref[held, :]], axis=0)
        out_ref[target * block : (target + 1) * block, :] = jnp.dot(
            chosen, lines, preferred_element_type=F32
        ).astype(BF16)


def in_order(near, far):
    rows, columns = 2 * near.shape[0], near.shape[1]
    return pl.pallas_call(
        order_kernel,
        out_shape=jax.ShapeDtypeStruct((rows, columns), BF16),
        in_specs=[whole(), whole()],
        out_specs=whole(),
        compiler_params=params(),
        cost_estimate=pl.CostEstimate(
            flops=2 * rows * rows * columns, transcendentals=0, bytes_accessed=4 * rows * columns
        ),
    )(near, far)


def prior_kernel(coef_ref, *refs):
    *features, out_ref = refs
    cands = features[0].shape[1]
    for chunk, feature_ref in enumerate(features):
        out_ref[:, chunk * cands : (chunk + 1) * cands] = jnp.dot(
            coef_ref[...], feature_ref[...], preferred_element_type=F32
        )


def cross_kernel(weight_ref, prior_ref, *refs):
    kernels, outs = refs[:-WIDTHS], refs[-WIDTHS:]
    block = weight_ref.shape[0] // WIDTHS
    cands = kernels[0].shape[1]
    for chunk, kernel_ref in enumerate(kernels):
        cols = slice(chunk * cands, (chunk + 1) * cands)
        total = prior_ref[:, cols] + jnp.dot(
            weight_ref[...], kernel_ref[...], preferred_element_type=F32
        )
        for target, out in enumerate(outs):
            rows = slice(target * block, (target + 1) * block)
            out[:, cols] = total[rows].astype(out.dtype)


def prior_product(coefs, features):
    rows, cands = coefs.shape[0], len(features) * features[0].shape[1]
    feats = coefs.shape[1]
    return pl.pallas_call(
        prior_kernel,
        out_shape=jax.ShapeDtypeStruct((rows, cands), F32),
        in_specs=[whole()] * (1 + len(features)),
        out_specs=whole(),
        compiler_params=params(),
        cost_estimate=pl.CostEstimate(
            flops=2 * rows * feats * cands, transcendentals=0, bytes_accessed=2 * feats * cands
        ),
    )(coefs, *features)


def cross_product(weights, prior, kernels):
    rows, cands = prior.shape
    obs = weights.shape[1]
    shape = (rows // WIDTHS, cands)
    out_shapes = (jax.ShapeDtypeStruct(shape, F32),) + (jax.ShapeDtypeStruct(shape, BF16),) * (
        WIDTHS - 1
    )
    return pl.pallas_call(
        cross_kernel,
        out_shape=out_shapes,
        in_specs=[whole()] * (2 + len(kernels)),
        out_specs=(whole(),) * WIDTHS,
        compiler_params=params(),
        cost_estimate=pl.CostEstimate(
            flops=2 * rows * obs * cands, transcendentals=0, bytes_accessed=8 * rows * cands
        ),
    )(weights, prior, *kernels)


def total_kernel(first, *refs):
    *parts, out_ref, sums, sem = refs
    total = parts[0][...]
    for part in parts[1:WIDTHS]:
        total = total + part[...].astype(F32)
    sums[...] = total
    copy = pltpu.make_async_copy(sums, out_ref.at[:, first : first + total.shape[1]], sem)
    copy.start()
    copy.wait()


def total(parts, first, cands, held):
    rows, columns = parts[0].shape
    extra = [] if held is None else [held]
    return pl.pallas_call(
        functools.partial(total_kernel, first),
        out_shape=jax.ShapeDtypeStruct((rows, cands), F32),
        in_specs=[whole()] * len(parts) + [pl.BlockSpec(memory_space=pl.ANY)] * len(extra),
        out_specs=pl.BlockSpec(memory_space=pl.ANY),
        scratch_shapes=[pltpu.VMEM((rows, columns), F32), pltpu.SemaphoreType.DMA(())],
        input_output_aliases={len(parts): 0} if extra else {},
        compiler_params=params(),
        cost_estimate=pl.CostEstimate(
            flops=3 * rows * columns, transcendentals=0, bytes_accessed=14 * rows * columns
        ),
    )(*parts, *extra)


def exchange_pairs(mask):
    devices = WIDTHS * DEPTHS * CORES
    return [(i, i ^ mask) for i in range(devices)]


def stack_kernel(*refs):
    *pieces, out_ref, rows = refs
    count = pieces[0].shape[0]
    if count % 16 == 0:
        for index, piece in enumerate(pieces):
            out_ref[index * count : (index + 1) * count, :] = piece[...]
        return
    for index, piece in enumerate(pieces):
        rows[index * count : (index + 1) * count, :] = piece[...].astype(F32)
    out_ref[...] = rows[...].astype(BF16)


def stack(pieces):
    shape = (len(pieces) * pieces[0].shape[0], pieces[0].shape[1])
    return pl.pallas_call(
        stack_kernel,
        out_shape=jax.ShapeDtypeStruct(shape, BF16),
        in_specs=[whole()] * len(pieces),
        out_specs=whole(),
        scratch_shapes=[pltpu.VMEM(shape, F32)],
        compiler_params=params(),
        cost_estimate=pl.CostEstimate(
            flops=0, transcendentals=0, bytes_accessed=4 * shape[0] * shape[1]
        ),
    )(*pieces)


def spread(piece, at_once):
    def swap(held, pairs):
        return lax.ppermute(held, "cand", pairs)

    held = piece
    for hop in (1, 2, 7):
        other = swap(held, exchange_pairs(hop * CORES))
        held = stack([held, other])
    step = DEPTHS * CORES
    if at_once:
        others = [swap(held, exchange_pairs(hop * step)) for hop in (1, 3, 2)]
        near = stack([held] + others)
    else:
        near = stack([held, swap(held, exchange_pairs(step))])
        near = stack([near, swap(near, exchange_pairs(3 * step))])
    return near, swap(near, exchange_pairs(1))


def exact_lines(left, lines):
    rows = left.shape[0]
    lines[...] = jnp.zeros_like(lines)
    for index, piece in enumerate(three_pieces(left)[:2]):
        lines[index * rows : (index + 1) * rows, :] = piece
    return lines[...].astype(BF16)


def exact_dot(lines, rows, right):
    high = right.astype(BF16)
    middle = (right - high.astype(F32)).astype(BF16)
    first = jnp.dot(lines, high, preferred_element_type=F32)
    second = jnp.dot(lines, middle, preferred_element_type=F32)
    return second[:rows] + first[rows : 2 * rows] + first[:rows]


def solve_kernel(
    section, whitened_ref, inverse_ref, factor_ref, carried_ref, weights_ref, *rest
):
    *update_ref, solved_ref, lines = rest
    count, width = whitened_ref.shape
    active = lax.axis_index("rows") == section

    @pl.when(active)
    def _():
        remaining = whitened_ref[...]
        if carried_ref is not None:
            remaining = remaining - carried_ref[:, section * width : (section + 1) * width]
        solved = exact_dot(exact_lines(remaining, lines), count, inverse_ref[...])
        solved_ref[...] = solved.astype(BF16)
        if section > 0:
            left = exact_lines(solved, lines)

            @pl.loop(0, section)
            def _(earlier):
                cols = pl.ds(pl.multiple_of(earlier * width, width), width)
                update = exact_dot(left, count, factor_ref[:, cols])
                if carried_ref is not None:
                    update = update + carried_ref[:, cols]
                update_ref[0][:, cols] = update

    if weights_ref is not None:
        @pl.when(jnp.logical_not(active))
        def _():
            solved_ref[...] = weights_ref[...]


def solve(section, whitened, carried, weights, diag_inv, factor_rows):
    count, width = whitened.shape
    out_shape = [jax.ShapeDtypeStruct((count, width), BF16)]
    if section > 0:
        out_shape.insert(0, jax.ShapeDtypeStruct((count, section * width), F32))
    first = carried is None

    def kernel(whitened_ref, inverse_ref, factor_ref, *refs):
        if first:
            refs = (None, None) + refs
        solve_kernel(section, whitened_ref, inverse_ref, factor_ref, *refs)

    held = [] if first else [carried, weights]
    columns = (section + 1) * width
    results = pl.pallas_call(
        kernel,
        out_shape=out_shape,
        in_specs=[whole()] * (3 + len(held)),
        out_specs=[whole()] * len(out_shape),
        scratch_shapes=[pltpu.VMEM((16, width), F32)],
        compiler_params=params(),
        cost_estimate=pl.CostEstimate(
            flops=2 * 32 * width * columns, transcendentals=0, bytes_accessed=4 * width * columns
        ),
    )(whitened, diag_inv, factor_rows, *held)
    return results if section > 0 else (None, results[0])


def solve_chain(whitened, factor_rows, diag_inv):
    sections = lax.axis_size("rows")
    carried = weights = None
    for section in reversed(range(sections)):
        carried, weights = solve(section, whitened, carried, weights, diag_inv, factor_rows)
        if section > 0:
            carried = lax.ppermute(carried, "rows", [(section, section - 1)])
    return weights


def body(
    whitened,
    factor_rows,
    diag_inv,
    observed,
    inv_length,
    grid_coords,
    frequencies,
    phases,
    prior_coef,
):
    turns, exponent, levels, inverse, factor = prepare(
        frequencies, phases, observed, inv_length, grid_coords, diag_inv, factor_rows
    )
    coef_near, coef_far = spread(prior_coef, False)
    weights = solve_chain(whitened, factor, inverse)
    weight_near, weight_far = spread(weights, True)
    made = [tiles(turns, exponent, levels, chunk) for chunk in range(CHUNKS)]
    coefs = in_order(coef_near, coef_far)
    solved = in_order(weight_near, weight_far)
    rows = lax.axis_size("rows")
    result = None
    for first, last in PARTS:
        mine = made[first:last]
        prior = prior_product(coefs, [m[0] for m in mine])
        own, *away = cross_product(solved, prior, [m[1] for m in mine])
        arrived = []
        for shift, block in enumerate(away, 1):
            pairs = [(i, (i + shift) % rows) for i in range(rows)]
            arrived.append(lax.ppermute(block, "rows", pairs))
        cands = grid_coords.shape[1]
        start = first * (cands // CHUNKS)
        result = total([own] + arrived, start, cands, result)
    return result.T


def solution(mesh):
    in_specs = (
        P("cand", "rows"),
        P("rows", None),
        P("rows", None),
        P(None, "rows"),
        P(),
        P(None, "cand"),
        P(None, "rows"),
        P("rows"),
        P("cand", "rows"),
    )
    out_specs = P("cand", "rows")

    return jax.shard_map(body, mesh=mesh, in_specs=in_specs, out_specs=out_specs, check_vma=False)
```

```python
import functools

import jax
import jax.numpy as jnp
from jax import lax
from jax.experimental import pallas as pl
from jax.experimental.pallas import tpu as pltpu
from jax.sharding import PartitionSpec as P

F32 = jnp.float32
BF16 = jnp.bfloat16
GRID = 21
DIM = 22
CORES = 2
DEPTHS = 8
WIDTHS = 4
LANES = 128
STRIPE = 24
ROW_CHUNK = 256
CAND_TILE = 256
CHUNKS = 8
PARTS = ((0, 5), (5, 8))
VMEM_BYTES = 16 * 2**20
LOG2E = 1.4426950408889634
INV_TURN = 0.15915494309189535
SINE = (0.55535848, -0.91343016, 0.4493464, -0.09804192)


def params(limit=VMEM_BYTES):
    return pltpu.CompilerParams(vmem_limit_bytes=limit)


def whole():
    return pl.BlockSpec(memory_space=pltpu.VMEM)


def three_pieces(values):
    high = values.astype(BF16).astype(F32)
    rest = values - high
    middle = rest.astype(BF16).astype(F32)
    return high, middle, (rest - middle).astype(BF16).astype(F32)


def stack_pieces(scratch, values, tail):
    scratch[...] = jnp.zeros_like(scratch)
    for piece, part in enumerate(values):
        scratch[piece * STRIPE : piece * STRIPE + DIM, :] = part
    row = lax.broadcasted_iota(jnp.int32, (8, scratch.shape[1]), 0)
    block = jnp.zeros((8, scratch.shape[1]), F32)
    for index, line in enumerate(tail):
        block = jnp.where(row == index, line, block)
    scratch[3 * STRIPE : 3 * STRIPE + 8, :] = block


def prepare_kernel(*refs):
    sources, refs = refs[:7], refs[7:]
    (turns_ref, exponent_ref, levels_ref, inverse_ref, factor_ref), refs = refs[:5], refs[5:]
    (freq_ref, phase_ref, observed_ref, scale_ref, grid_ref), refs = refs[:5], refs[5:]
    wide, narrow, tall, sems = refs
    targets = (freq_ref, phase_ref, observed_ref, scale_ref, grid_ref, inverse_ref, factor_ref)
    copies = [
        pltpu.make_async_copy(
            source.at[:, : target.shape[1]], target, sems.at[index]
        )
        for index, (source, target) in enumerate(zip(sources, targets))
    ]
    for copy in copies:
        copy.start()
    for copy in copies[:5]:
        copy.wait()
    stack_pieces(
        wide,
        three_pieces(freq_ref[...] * (INV_TURN / (GRID - 1))),
        three_pieces(phase_ref[...] * INV_TURN),
    )
    for start in range(0, wide.shape[1], 512):
        turns_ref[start : start + 512, :] = wide[:, start : start + 512].T.astype(BF16)
    scale = jnp.broadcast_to(scale_ref[...], (DIM, DIM))
    line = lax.broadcasted_iota(jnp.int32, (DIM, DIM), 0)
    lane = lax.broadcasted_iota(jnp.int32, (DIM, DIM), 1)
    scale = jnp.sum(jnp.where(line == lane, scale, 0.0), axis=1, keepdims=True)
    squares = scale * scale
    observed = observed_ref[...]
    ones = jnp.ones((1, narrow.shape[1]), F32)
    norm = jnp.sum(observed * observed * squares, axis=0, keepdims=True) * (-0.5 * LOG2E)
    stack_pieces(
        narrow,
        three_pieces(observed * squares * (LOG2E / (GRID - 1))),
        three_pieces(norm) + (ones, ones, ones),
    )
    exponent_ref[...] = narrow[...].T.astype(BF16)
    levels = grid_ref[...].astype(F32)
    ones = jnp.ones((1, tall.shape[1]), F32)
    norm = jnp.sum(levels * levels * squares, axis=0, keepdims=True) * (
        -0.5 * LOG2E / (GRID - 1) ** 2
    )
    stack_pieces(tall, (levels, levels, levels), (ones, ones, ones) + three_pieces(norm))
    levels_ref[...] = tall[...].astype(BF16)
    for copy in copies[5:]:
        copy.wait()


def prepare(frequencies, phases, observed, inv_length, grid_coords, diag_inv, factor_rows):
    feats, obs, cands = frequencies.shape[1], observed.shape[1], grid_coords.shape[1]
    arrays = (frequencies, phases[None, :], observed, inv_length[None, :], grid_coords)
    earlier = factor_rows.shape[1] - diag_inv.shape[1]
    return pl.pallas_call(
        prepare_kernel,
        out_shape=(
            jax.ShapeDtypeStruct((feats, LANES), BF16),
            jax.ShapeDtypeStruct((obs, LANES), BF16),
            jax.ShapeDtypeStruct((LANES, cands), BF16),
            jax.ShapeDtypeStruct(diag_inv.shape, F32),
            jax.ShapeDtypeStruct((factor_rows.shape[0], earlier), F32),
        ),
        in_specs=[pl.BlockSpec(memory_space=pl.ANY)] * 7,
        out_specs=(whole(),) * 5,
        scratch_shapes=[pltpu.VMEM(array.shape, array.dtype) for array in arrays]
        + [
            pltpu.VMEM((LANES, feats), F32),
            pltpu.VMEM((LANES, obs), F32),
            pltpu.VMEM((LANES, cands), F32),
            pltpu.SemaphoreType.DMA((7,)),
        ],
        compiler_params=params(),
        cost_estimate=pl.CostEstimate(flops=10**7, transcendentals=0, bytes_accessed=8 * 2**20),
        name="prepare",
    )(
        *(
            pltpu.with_memory_space_constraint(array, pltpu.HBM)
            for array in (*arrays, diag_inv, factor_rows)
        )
    )


def cosine(turns):
    near = turns - jnp.round(turns)
    square = near * near
    poly = ((SINE[3] * square + SINE[2]) * square + SINE[1]) * square + SINE[0]
    sine = near * poly
    return (0.015625 - sine * sine).astype(BF16)


def tile_kernel(first, turns_ref, exponent_ref, levels_ref, features_ref, kernel_ref):
    @pl.loop(0, features_ref.shape[1] // CAND_TILE)
    def _(tile):
        start = pl.multiple_of(tile * CAND_TILE, CAND_TILE)
        cols = pl.ds(start, CAND_TILE)
        levels = levels_ref[:, pl.ds(pl.multiple_of(first + start, CAND_TILE), CAND_TILE)]
        for start in range(0, turns_ref.shape[0], ROW_CHUNK):
            rows = slice(start, start + ROW_CHUNK)
            turns = jnp.dot(turns_ref[rows, :], levels, preferred_element_type=F32)
            features_ref[rows, cols] = cosine(turns)
        for start in range(0, exponent_ref.shape[0], ROW_CHUNK):
            rows = slice(start, start + ROW_CHUNK)
            exponent = jnp.dot(exponent_ref[rows, :], levels, preferred_element_type=F32)
            kernel_ref[rows, cols] = jnp.exp2(exponent).astype(BF16)


def tiles(turns, exponent, levels, chunk):
    feats, obs = turns.shape[0], exponent.shape[0]
    cands = levels.shape[1] // CHUNKS
    return pl.pallas_call(
        functools.partial(tile_kernel, chunk * cands),
        out_shape=(
            jax.ShapeDtypeStruct((feats, cands), BF16),
            jax.ShapeDtypeStruct((obs, cands), BF16),
        ),
        in_specs=[whole()] * 3,
        out_specs=(whole(),) * 2,
        compiler_params=params(),
        cost_estimate=pl.CostEstimate(
            flops=24 * (feats + obs) * cands,
            transcendentals=obs * cands,
            bytes_accessed=2 * (feats + obs) * cands,
        ),
    )(turns, exponent, levels)


def order_kernel(near_ref, far_ref, out_ref):
    rows, half = out_ref.shape[0], near_ref.shape[0] // WIDTHS
    block = rows // WIDTHS
    shard = rows // (WIDTHS * DEPTHS * CORES)
    across, mine = lax.axis_index("rows"), lax.axis_index("cand")
    row = lax.broadcasted_iota(jnp.int32, (block, block), 0)
    column = lax.broadcasted_iota(jnp.int32, (block, block), 1)
    offset = (row // shard) ^ (mine & (DEPTHS * CORES - 1))
    depth = offset // CORES
    depth = jnp.where(depth < DEPTHS // 2, depth, depth ^ (DEPTHS // 2 - 1))
    source = ((offset & (CORES - 1)) * DEPTHS + depth) * shard + (row & (shard - 1))
    chosen = (source == column).astype(F32).astype(BF16)
    for target in range(WIDTHS):
        width = ((across + target) & (WIDTHS - 1)) ^ (mine // (DEPTHS * CORES))
        width = width ^ (width // 2)
        held = pl.ds(pl.multiple_of(width * half, half), half)
        lines = jnp.concatenate([near_ref[held, :], far_ref[held, :]], axis=0)
        out_ref[target * block : (target + 1) * block, :] = jnp.dot(
            chosen, lines, preferred_element_type=F32
        ).astype(BF16)


def in_order(near, far):
    rows, columns = 2 * near.shape[0], near.shape[1]
    return pl.pallas_call(
        order_kernel,
        out_shape=jax.ShapeDtypeStruct((rows, columns), BF16),
        in_specs=[whole(), whole()],
        out_specs=whole(),
        compiler_params=params(),
        cost_estimate=pl.CostEstimate(
            flops=2 * rows * rows * columns, transcendentals=0, bytes_accessed=4 * rows * columns
        ),
    )(near, far)


def prior_kernel(coef_ref, *refs):
    *features, out_ref = refs
    cands = features[0].shape[1]
    for chunk, feature_ref in enumerate(features):
        out_ref[:, chunk * cands : (chunk + 1) * cands] = jnp.dot(
            coef_ref[...], feature_ref[...], preferred_element_type=F32
        )


def cross_kernel(weight_ref, prior_ref, *refs):
    kernels, outs = refs[:-WIDTHS], refs[-WIDTHS:]
    block = weight_ref.shape[0] // WIDTHS
    cands = kernels[0].shape[1]
    for chunk, kernel_ref in enumerate(kernels):
        cols = slice(chunk * cands, (chunk + 1) * cands)
        total = prior_ref[:, cols] + jnp.dot(
            weight_ref[...], kernel_ref[...], preferred_element_type=F32
        )
        for target, out in enumerate(outs):
            rows = slice(target * block, (target + 1) * block)
            out[:, cols] = total[rows].astype(out.dtype)


def prior_product(coefs, features):
    rows, cands = coefs.shape[0], len(features) * features[0].shape[1]
    feats = coefs.shape[1]
    return pl.pallas_call(
        prior_kernel,
        out_shape=jax.ShapeDtypeStruct((rows, cands), F32),
        in_specs=[whole()] * (1 + len(features)),
        out_specs=whole(),
        compiler_params=params(),
        cost_estimate=pl.CostEstimate(
            flops=2 * rows * feats * cands, transcendentals=0, bytes_accessed=2 * feats * cands
        ),
    )(coefs, *features)


def cross_product(weights, prior, kernels):
    rows, cands = prior.shape
    obs = weights.shape[1]
    shape = (rows // WIDTHS, cands)
    out_shapes = (jax.ShapeDtypeStruct(shape, F32),) + (jax.ShapeDtypeStruct(shape, BF16),) * (
        WIDTHS - 1
    )
    return pl.pallas_call(
        cross_kernel,
        out_shape=out_shapes,
        in_specs=[whole()] * (2 + len(kernels)),
        out_specs=(whole(),) * WIDTHS,
        compiler_params=params(),
        cost_estimate=pl.CostEstimate(
            flops=2 * rows * obs * cands, transcendentals=0, bytes_accessed=8 * rows * cands
        ),
    )(weights, prior, *kernels)


def total_kernel(first, *refs):
    *parts, out_ref, sums, sem = refs
    total = parts[0][...]
    for part in parts[1:WIDTHS]:
        total = total + part[...].astype(F32)
    sums[...] = total
    copy = pltpu.make_async_copy(sums, out_ref.at[:, first : first + total.shape[1]], sem)
    copy.start()
    copy.wait()


def total(parts, first, cands, held):
    rows, columns = parts[0].shape
    extra = [] if held is None else [held]
    return pl.pallas_call(
        functools.partial(total_kernel, first),
        out_shape=jax.ShapeDtypeStruct((rows, cands), F32),
        in_specs=[whole()] * len(parts) + [pl.BlockSpec(memory_space=pl.ANY)] * len(extra),
        out_specs=pl.BlockSpec(memory_space=pl.ANY),
        scratch_shapes=[pltpu.VMEM((rows, columns), F32), pltpu.SemaphoreType.DMA(())],
        input_output_aliases={len(parts): 0} if extra else {},
        compiler_params=params(),
        cost_estimate=pl.CostEstimate(
            flops=3 * rows * columns, transcendentals=0, bytes_accessed=14 * rows * columns
        ),
    )(*parts, *extra)


def exchange_pairs(mask):
    devices = WIDTHS * DEPTHS * CORES
    return [(i, i ^ mask) for i in range(devices)]


def stack_kernel(*refs):
    *pieces, out_ref, rows = refs
    count = pieces[0].shape[0]
    if count % 16 == 0:
        for index, piece in enumerate(pieces):
            out_ref[index * count : (index + 1) * count, :] = piece[...]
        return
    for index, piece in enumerate(pieces):
        rows[index * count : (index + 1) * count, :] = piece[...].astype(F32)
    out_ref[...] = rows[...].astype(BF16)


def stack(pieces):
    shape = (len(pieces) * pieces[0].shape[0], pieces[0].shape[1])
    return pl.pallas_call(
        stack_kernel,
        out_shape=jax.ShapeDtypeStruct(shape, BF16),
        in_specs=[whole()] * len(pieces),
        out_specs=whole(),
        scratch_shapes=[pltpu.VMEM(shape, F32)],
        compiler_params=params(),
        cost_estimate=pl.CostEstimate(
            flops=0, transcendentals=0, bytes_accessed=4 * shape[0] * shape[1]
        ),
    )(*pieces)


def spread(piece, at_once):
    def swap(held, pairs):
        return lax.ppermute(held, "cand", pairs)

    held = piece
    for hop in (1, 2, 7):
        other = swap(held, exchange_pairs(hop * CORES))
        held = stack([held, other])
    step = DEPTHS * CORES
    if at_once:
        others = [swap(held, exchange_pairs(hop * step)) for hop in (1, 3, 2)]
        near = stack([held] + others)
    else:
        near = stack([held, swap(held, exchange_pairs(step))])
        near = stack([near, swap(near, exchange_pairs(3 * step))])
    return near, swap(near, exchange_pairs(1))


def exact_lines(left, lines):
    rows = left.shape[0]
    lines[...] = jnp.zeros_like(lines)
    for index, piece in enumerate(three_pieces(left)[:2]):
        lines[index * rows : (index + 1) * rows, :] = piece
    return lines[...].astype(BF16)


def exact_dot(lines, rows, right):
    high = right.astype(BF16)
    middle = (right - high.astype(F32)).astype(BF16)
    first = jnp.dot(lines, high, preferred_element_type=F32)
    second = jnp.dot(lines, middle, preferred_element_type=F32)
    return second[:rows] + first[rows : 2 * rows] + first[:rows]


def solve_kernel(
    section, whitened_ref, inverse_ref, factor_ref, carried_ref, weights_ref, *rest
):
    *update_ref, solved_ref, lines = rest
    count, width = whitened_ref.shape
    active = lax.axis_index("rows") == section

    @pl.when(active)
    def _():
        remaining = whitened_ref[...]
        if carried_ref is not None:
            remaining = remaining - carried_ref[:, section * width : (section + 1) * width]
        solved = exact_dot(exact_lines(remaining, lines), count, inverse_ref[...])
        solved_ref[...] = solved.astype(BF16)
        if section > 0:
            left = exact_lines(solved, lines)

            @pl.loop(0, section)
            def _(earlier):
                cols = pl.ds(pl.multiple_of(earlier * width, width), width)
                update = exact_dot(left, count, factor_ref[:, cols])
                if carried_ref is not None:
                    update = update + carried_ref[:, cols]
                update_ref[0][:, cols] = update

    if weights_ref is not None:
        @pl.when(jnp.logical_not(active))
        def _():
            solved_ref[...] = weights_ref[...]


def solve(section, whitened, carried, weights, diag_inv, factor_rows):
    count, width = whitened.shape
    out_shape = [jax.ShapeDtypeStruct((count, width), BF16)]
    if section > 0:
        out_shape.insert(0, jax.ShapeDtypeStruct((count, section * width), F32))
    first = carried is None

    def kernel(whitened_ref, inverse_ref, factor_ref, *refs):
        if first:
            refs = (None, None) + refs
        solve_kernel(section, whitened_ref, inverse_ref, factor_ref, *refs)

    held = [] if first else [carried, weights]
    columns = (section + 1) * width
    results = pl.pallas_call(
        kernel,
        out_shape=out_shape,
        in_specs=[whole()] * (3 + len(held)),
        out_specs=[whole()] * len(out_shape),
        scratch_shapes=[pltpu.VMEM((16, width), F32)],
        compiler_params=params(),
        cost_estimate=pl.CostEstimate(
            flops=2 * 32 * width * columns, transcendentals=0, bytes_accessed=4 * width * columns
        ),
    )(whitened, diag_inv, factor_rows, *held)
    return results if section > 0 else (None, results[0])


def solve_chain(whitened, factor_rows, diag_inv):
    sections = lax.axis_size("rows")
    carried = weights = None
    for section in reversed(range(sections)):
        carried, weights = solve(section, whitened, carried, weights, diag_inv, factor_rows)
        if section > 0:
            carried = lax.ppermute(carried, "rows", [(section, section - 1)])
    return weights


def body(
    whitened,
    factor_rows,
    diag_inv,
    observed,
    inv_length,
    grid_coords,
    frequencies,
    phases,
    prior_coef,
):
    turns, exponent, levels, inverse, factor = prepare(
        frequencies, phases, observed, inv_length, grid_coords, diag_inv, factor_rows
    )
    coef_near, coef_far = spread(prior_coef, False)
    weights = solve_chain(whitened, factor, inverse)
    weight_near, weight_far = spread(weights, True)
    made = [tiles(turns, exponent, levels, chunk) for chunk in range(CHUNKS)]
    coefs = in_order(coef_near, coef_far)
    solved = in_order(weight_near, weight_far)
    rows = lax.axis_size("rows")
    result = None
    for first, last in PARTS:
        mine = made[first:last]
        prior = prior_product(coefs, [m[0] for m in mine])
        own, *away = cross_product(solved, prior, [m[1] for m in mine])
        arrived = []
        for shift, block in enumerate(away, 1):
            pairs = [(i, (i + shift) % rows) for i in range(rows)]
            arrived.append(lax.ppermute(block, "rows", pairs))
        cands = grid_coords.shape[1]
        start = first * (cands // CHUNKS)
        result = total([own] + arrived, start, cands, result)
    return result.T


def solution(mesh):
    in_specs = (
        P("cand", "rows"),
        P("rows", None),
        P("rows", None),
        P(None, "rows"),
        P(),
        P(None, "cand"),
        P(None, "rows"),
        P("rows"),
        P("cand", "rows"),
    )
    out_specs = P("cand", "rows")

    return jax.shard_map(body, mesh=mesh, in_specs=in_specs, out_specs=out_specs, check_vma=False)
```
